32 devices in a mesh: fsdp: 2 (over x), heads: 4 (over y, core), tensor: 4 (over z).
Axes of the slice: x: 2, y: 2, z: 4, core: 2. Of those that a mesh axis runs over, the one named last changes fastest.
Arguments:
- block_input: bfloat16 [4096, 2048], P(('fsdp', 'tensor')), may hold values from -6 to 6
- cotangent: bfloat16 [4096, 2048], P(('fsdp', 'tensor')), may hold values from -6 to 6
- norm1_gain: float32 [2048], replicated, may hold values from 0.25 to 1.75
- latent_gain: float32 [512], replicated, may hold values from 0.25 to 1.75
- norm2_gain: float32 [2048], replicated, may hold values from 0.25 to 1.75
- w_query: bfloat16 [2048, 3072], P(('fsdp', 'tensor'), 'heads'), may hold values from -0.125 to 0.125
- w_latent: bfloat16 [2048, 576], P(('fsdp', 'tensor')), may hold values from -0.125 to 0.125
- w_kv: bfloat16 [512, 4096], P(('fsdp', 'tensor'), 'heads'), may hold values from -0.25 to 0.25
- w_out: bfloat16 [2048, 2048], P('heads', ('fsdp', 'tensor')), may hold values from -0.5 to 0.5
- expert_gate: bfloat16 [16, 2048, 1408], P(('fsdp', 'heads'), None, 'tensor'), may hold values from -0.125 to 0.125
- expert_up: bfloat16 [16, 2048, 1408], P(('fsdp', 'heads'), None, 'tensor'), may hold values from -0.125 to 0.125
- expert_down: bfloat16 [16, 1408, 2048], P(('fsdp', 'heads'), 'tensor'), may hold values from -0.15625 to 0.15625
- shared_gate: bfloat16 [2048, 2816], P(('fsdp', 'heads'), 'tensor'), may hold values from -0.125 to 0.125
- shared_up: bfloat16 [2048, 2816], P(('fsdp', 'heads'), 'tensor'), may hold values from -0.125 to 0.125
- shared_down: bfloat16 [2816, 2048], P('tensor', ('fsdp', 'heads')), may hold values from -0.109375 to 0.109375
- routed_expert_index: int32 [4096, 6], P(('fsdp', 'tensor')), may hold values from 0 to 15, as said below
- slots: int32 [4096, 6], P(('fsdp', 'tensor')), may hold values from 0 to 240, as said below
- gate_weights: bfloat16 [4096, 6], P(('fsdp', 'tensor')), may hold values from 0.049804688 to 0.5
Outputs:
- output: bfloat16 [4096, 2048], P(('fsdp', 'tensor'))
- input_grad: float32 [4096, 2048], P(('fsdp', 'tensor'))
- norm1_gain_grad: float32 [2048], P(('fsdp', 'tensor'))
- latent_gain_grad: float32 [512], P(('fsdp', 'tensor'))
- norm2_gain_grad: float32 [2048], P(('fsdp', 'tensor'))
- w_query_grad: float32 [2048, 3072], P(('fsdp', 'tensor'), 'heads')
- w_latent_grad: float32 [2048, 576], P(('fsdp', 'tensor'))
- w_kv_grad: float32 [512, 4096], P(('fsdp', 'tensor'), 'heads')
- w_out_grad: float32 [2048, 2048], P('heads', ('fsdp', 'tensor'))
- expert_gate_grad: float32 [16, 2048, 1408], P(('fsdp', 'heads'), None, 'tensor')
- expert_up_grad: float32 [16, 2048, 1408], P(('fsdp', 'heads'), None, 'tensor')
- expert_down_grad: float32 [16, 1408, 2048], P(('fsdp', 'heads'), 'tensor')
- shared_gate_grad: float32 [2048, 2816], P(('fsdp', 'heads'), 'tensor')
- shared_up_grad: float32 [2048, 2816], P(('fsdp', 'heads'), 'tensor')
- shared_down_grad: float32 [2816, 2048], P('tensor', ('fsdp', 'heads'))
The draws below stay inside these ranges and needn't reach their ends.
Inputs may be any that keep to these rules, and one draw needn't show every extreme that they name: `routed_expert_index`: each row names 6 different experts. In every routing block (f, h), the rows f * 2048 + t * 512 + h * 128 + i, one expert is named by every row. `slots`: A route's slot is the number of earlier routes of its routing block to the same expert, in the order of place t * 128 + i and then of the route's position, with 240 for every route beyond the first 240; 240 marks a dropped route, so each used (expert, slot) pair of a block appears once.
All inputs are finite; a program needn't handle non-finite values.
Results may differ from the reference program's by a relative error of at most 0.024.
Values may be sent and summed in bfloat16 or wider, within the bound.
No kernel may reach another device: no remote copies, remote signals or barrier semaphores. Data moves between devices by JAX's collectives and lax.ppermute only.
A program may use at most 384 MiB of HBM per device.

```python
import math
import jax
import jax.numpy as jnp
from jax import lax

D = 2048
HEADS = 16
NOPE = 128
ROPE = 64
VDIM = 128
KVR = 512
FF = 1408
SHARED = 2
TOP = 6
LEN = 512
QROWS = 128
BLOCK_ROWS = 512
TOKENS = 4096
EXPERTS = 16
CAP = 240
N_FSDP = 2
N_HEADS = 4
N_TENSOR = 4


def routing(base_key):
    base_key = jax.random.fold_in(base_key, 11)
    key_one, key_two, key_three = jax.random.split(base_key, 3)
    blocks = N_FSDP * N_HEADS
    noise_draw = jax.random.randint(key_one, (blocks, BLOCK_ROWS, EXPERTS), 0, 1024)
    bonuses = jax.random.randint(key_two, (blocks, 1, EXPERTS), 0, 512)
    favored = jax.random.randint(key_three, (blocks, 1, 1), 0, EXPERTS)
    labels = jnp.arange(EXPERTS, dtype=jnp.int32)
    scores = (noise_draw + bonuses + 4096 * (labels == favored).astype(jnp.int32)) * EXPERTS + labels
    chosen = lax.top_k(scores, TOP)[1].astype(jnp.int32)
    flattened = chosen.reshape(blocks, BLOCK_ROWS * TOP)
    one_hot = (flattened[:, :, None] == labels).astype(jnp.int32)
    earlier = jnp.cumsum(one_hot, axis=1) - one_hot
    ranking = jnp.sum(earlier * one_hot, axis=2)
    slot_index = jnp.minimum(ranking, CAP).reshape(blocks, BLOCK_ROWS, TOP)

    def reorder(array):
        shaped = array.reshape(N_FSDP, N_HEADS, N_TENSOR, QROWS, TOP)
        return jnp.transpose(shaped, (0, 2, 1, 3, 4)).reshape(N_FSDP * N_TENSOR * N_HEADS * QROWS, TOP)
    return (reorder(chosen), reorder(slot_index))


def draw_routed_expert_index(key, part):
    return routing(key)[0]


def draw_slots(key, part):
    return routing(key)[1]


def shard_levels(key, shape, cuts, smallest, largest):
    def one(dim, shards_of):
        draws = jax.random.uniform(jax.random.fold_in(jax.random.fold_in(key, 6), dim), (shards_of,), jnp.float32, smallest / len(cuts), largest / len(cuts))
        return jnp.repeat(jnp.exp(draws), shape[dim] // shards_of).reshape((-1,) + (1,) * (len(shape) - dim - 1))

    factor_of = one(*cuts[0])
    for cut in cuts[1:]:
        factor_of = factor_of * one(*cut)
    return factor_of


def scatter_about(rng, extent, spread, bound, cuts=(), kind=jnp.bfloat16):
    factor_of = shard_levels(rng, extent, cuts, -0.22, 0.18) if cuts else 1.0
    drawn = jax.random.normal(rng, extent, jnp.float32) * spread * factor_of
    return jnp.minimum(jnp.maximum(drawn, -bound), bound).astype(kind)


def setup_inputs(seed: int = 0) -> dict:
    seeds = jax.random.split(jax.random.key(seed), 19)
    block_input = scatter_about(seeds[0], (TOKENS, D), 1.0, 6.0, ((0, 8),))
    cotangent = scatter_about(seeds[1], (TOKENS, D), 1.0, 6.0, ((0, 8),))
    norm1_gain = jnp.clip(1.0 + 0.15 * jax.random.normal(seeds[2], (D,), jnp.float32), 0.25, 1.75)
    latent_gain = jnp.clip(1.0 + 0.15 * jax.random.normal(seeds[3], (KVR,), jnp.float32), 0.25, 1.75)
    norm2_gain = jnp.clip(1.0 + 0.15 * jax.random.normal(seeds[4], (D,), jnp.float32), 0.25, 1.75)
    w_query = scatter_about(seeds[5], (D, HEADS * (NOPE + ROPE)), D ** -0.5, 0.125, ((0, 8), (1, 4)))
    w_latent = scatter_about(seeds[6], (D, KVR + ROPE), D ** -0.5, 0.125, ((0, 8),))
    w_kv = scatter_about(seeds[7], (KVR, HEADS * (NOPE + VDIM)), KVR ** -0.5, 0.25, ((0, 8), (1, 4)))
    w_out = scatter_about(seeds[8], (HEADS * VDIM, D), (HEADS * VDIM // 16) ** -0.5, 0.5, ((0, 4), (1, 8)))
    expert_gate = scatter_about(seeds[9], (EXPERTS, D, FF), D ** -0.5, 0.125, ((0, 8), (2, 4)))
    expert_up = scatter_about(seeds[10], (EXPERTS, D, FF), D ** -0.5, 0.125, ((0, 8), (2, 4)))
    expert_down = scatter_about(seeds[11], (EXPERTS, FF, D), FF ** -0.5, 0.15625, ((0, 8), (1, 4)))
    shared_gate = scatter_about(seeds[12], (D, SHARED * FF), D ** -0.5, 0.125, ((0, 8), (1, 4)))
    shared_up = scatter_about(seeds[13], (D, SHARED * FF), D ** -0.5, 0.125, ((0, 8), (1, 4)))
    shared_down = scatter_about(seeds[14], (SHARED * FF, D), (SHARED * FF) ** -0.5, 0.109375, ((0, 4), (1, 8)))
    routed_expert_index = draw_routed_expert_index(jax.random.fold_in(seeds[18], 71), 0)
    slots = draw_slots(jax.random.fold_in(seeds[18], 71), 0)
    gate_weights = jnp.clip(jnp.exp(math.log(0.5) - 2.306499 * jax.random.uniform(seeds[17], (TOKENS, TOP), jnp.float32) ** shard_levels(seeds[17], (TOKENS, TOP), ((0, 8),), -0.2, 0.2)), 0.049804688, 0.5).astype(jnp.bfloat16)
    return dict(block_input=block_input, cotangent=cotangent, norm1_gain=norm1_gain, latent_gain=latent_gain, norm2_gain=norm2_gain, w_query=w_query, w_latent=w_latent, w_kv=w_kv, w_out=w_out, expert_gate=expert_gate, expert_up=expert_up, expert_down=expert_down, shared_gate=shared_gate, shared_up=shared_up, shared_down=shared_down, routed_expert_index=routed_expert_index, slots=slots, gate_weights=gate_weights)


epsilon = 1e-06
theta_base = 10000.0
highest = lax.Precision.HIGHEST

@jax.custom_vjp
def low(v):
    return lax.optimization_barrier(v.astype(jnp.bfloat16)).astype(jnp.float32)

@jax.custom_vjp
def low_back(v):
    return v

def low_keep(v):
    return (low(v), None)

def low_pass(kept, grad):
    return (grad,)

def back_keep(v):
    return (v, None)

def back_low(kept, grad):
    return (low(grad),)
low.defvjp(low_keep, low_pass)
low_back.defvjp(back_keep, back_low)

def matmul(left, right):
    return jnp.dot(left, right, precision=highest, preferred_element_type=jnp.float32)

def rms_norm(vector, gain_vec):
    inverse = lax.rsqrt(lax.optimization_barrier(jnp.mean(vector * vector, axis=-1, keepdims=True)) + epsilon)
    return vector * inverse * gain_vec

def rope_tables(row_count):
    half_width = ROPE // 2
    position = (jnp.arange(row_count) % LEN).astype(jnp.float32)
    exponent = jnp.arange(half_width).astype(jnp.float32) * (2.0 / ROPE)
    frequency = theta_base ** (-exponent)
    angles = position[:, None] * frequency[None, :]
    return (jnp.cos(angles), jnp.sin(angles))

def rotate(vector, cosine, sine_table):
    half_width = vector.shape[-1] // 2
    first_half = vector[..., :half_width]
    second_half = vector[..., half_width:]
    return jnp.concatenate([first_half * cosine - second_half * sine_table, second_half * cosine + first_half * sine_table], axis=-1)

def silu(vector):
    return vector * jax.nn.sigmoid(vector)

def to_blocks(array):
    trailing = array.shape[1:]
    shaped = array.reshape((N_FSDP, N_TENSOR, N_HEADS, QROWS) + trailing)
    return jnp.swapaxes(shaped, 1, 2).reshape((N_FSDP * N_HEADS, N_TENSOR * QROWS) + trailing)

def from_blocks(array):
    trailing = array.shape[2:]
    shaped = array.reshape((N_FSDP, N_HEADS, N_TENSOR, QROWS) + trailing)
    return jnp.swapaxes(shaped, 1, 2).reshape((N_FSDP * N_TENSOR * N_HEADS * QROWS,) + trailing)

def expert_layer(block_input, norm1_gain, latent_gain, norm2_gain, w_query, w_latent, w_kv, w_out, expert_gate, expert_up, expert_down, shared_gate, shared_up, shared_down, routed_expert_index, slots, routing_gate_weights):
    token_count = block_input.shape[0]
    head_dim = NOPE + ROPE
    score_scale = head_dim ** (-0.5)
    first_input = low(rms_norm(block_input, norm1_gain))
    cosine, sine_table = rope_tables(token_count)
    query_raw = low_back(matmul(first_input, w_query)).reshape(token_count, HEADS, head_dim)
    queries = low(jnp.concatenate([query_raw[..., :NOPE], rotate(query_raw[..., NOPE:], cosine[:, None, :], sine_table[:, None, :])], axis=-1))
    latent_raw = low_back(matmul(first_input, w_latent))
    latent_norm = low(rms_norm(latent_raw[:, :KVR], latent_gain))
    key_rope = low(rotate(latent_raw[:, KVR:], cosine, sine_table))
    key_value = low(low_back(matmul(latent_norm, w_kv))).reshape(token_count, HEADS, NOPE + VDIM)
    key_all = jnp.concatenate([key_value[..., :NOPE], jnp.broadcast_to(key_rope[:, None, :], (token_count, HEADS, ROPE))], axis=-1)
    values = key_value[..., NOPE:]
    sequences = token_count // LEN
    group_size = 8 if sequences % 8 == 0 else 1
    causal = jnp.arange(LEN)[:, None] >= jnp.arange(LEN)[None, :]

    def attend(pieces):
        queries_g, keys_g, values_g = pieces
        scores = low_back(jnp.einsum('bqhd,bkhd->bhqk', queries_g, keys_g, precision=highest) * score_scale)
        scores = jnp.where(causal, scores, -1e+30)
        shifted = jnp.exp(scores - lax.optimization_barrier(jnp.max(scores, axis=-1, keepdims=True)))
        probabilities = low(shifted / lax.optimization_barrier(jnp.sum(shifted, axis=-1, keepdims=True)))
        return low(low_back(jnp.einsum('bhqk,bkhd->bqhd', probabilities, values_g, precision=highest)))
    outer = sequences // group_size
    context = lax.map(jax.checkpoint(attend), (queries.reshape(outer, group_size, LEN, HEADS, head_dim), key_all.reshape(outer, group_size, LEN, HEADS, head_dim), values.reshape(outer, group_size, LEN, HEADS, VDIM)))
    context = context.reshape(token_count, HEADS * VDIM)
    after_attention = block_input + low_back(matmul(context, w_out))
    second_input = low(rms_norm(after_attention, norm2_gain))

    def moe_block(pieces):
        rows_block, ids_block, slots_block, gates_block = pieces
        position = jnp.where(slots_block < CAP, ids_block * CAP + slots_block, EXPERTS * CAP).reshape(-1)
        source = jnp.broadcast_to(rows_block[:, None, :], (BLOCK_ROWS, TOP, D)).reshape(BLOCK_ROWS * TOP, D)
        buffer = jnp.zeros((EXPERTS * CAP + 1, D), jnp.float32).at[position].add(source)[:EXPERTS * CAP].reshape(EXPERTS, CAP, D)
        gate_act = low_back(jnp.einsum('ecd,edf->ecf', buffer, expert_gate, precision=highest))
        up_act = low_back(jnp.einsum('ecd,edf->ecf', buffer, expert_up, precision=highest))
        expert_hidden = low(silu(gate_act) * up_act)
        expert_out = low_back(jnp.einsum('ecf,efd->ecd', expert_hidden, expert_down, precision=highest))
        padded = jnp.concatenate([expert_out.reshape(EXPERTS * CAP, D), jnp.zeros((1, D), jnp.float32)], axis=0)
        picked = padded[position].reshape(BLOCK_ROWS, TOP, D)
        return lax.optimization_barrier(jnp.sum(picked * gates_block[:, :, None], axis=1))
    routed = from_blocks(lax.map(jax.checkpoint(moe_block), (to_blocks(second_input), to_blocks(routed_expert_index), to_blocks(slots), to_blocks(routing_gate_weights))))
    shared_act = low_back(matmul(second_input, shared_gate))
    shared_lin = low_back(matmul(second_input, shared_up))
    shared_hidden = low(silu(shared_act) * shared_lin)
    shared_out = matmul(shared_hidden, shared_down)
    return after_attention + routed + shared_out

def reference(block_input, cotangent, norm1_gain, latent_gain, norm2_gain, w_query, w_latent, w_kv, w_out, expert_gate, expert_up, expert_down, shared_gate, shared_up, shared_down, routed_expert_index, slots, gate_weights):
    routing_gate_weights = gate_weights.astype(jnp.float32)

    def forward_pass(layer_input_rows, first_norm_scale, latent_norm_scale, second_norm_scale, query_matrix, latent_matrix, key_value_matrix, output_matrix, expert_gate_matrix, expert_up_matrix, expert_down_matrix, shared_gate_matrix, shared_up_matrix, shared_down_matrix):
        return expert_layer(layer_input_rows, first_norm_scale, latent_norm_scale, second_norm_scale, query_matrix, latent_matrix, key_value_matrix, output_matrix, expert_gate_matrix, expert_up_matrix, expert_down_matrix, shared_gate_matrix, shared_up_matrix, shared_down_matrix, routed_expert_index, slots, routing_gate_weights)
    output, pullback = jax.vjp(forward_pass, block_input.astype(jnp.float32), norm1_gain.astype(jnp.float32), latent_gain.astype(jnp.float32), norm2_gain.astype(jnp.float32), w_query.astype(jnp.float32), w_latent.astype(jnp.float32), w_kv.astype(jnp.float32), w_out.astype(jnp.float32), expert_gate.astype(jnp.float32), expert_up.astype(jnp.float32), expert_down.astype(jnp.float32), shared_gate.astype(jnp.float32), shared_up.astype(jnp.float32), shared_down.astype(jnp.float32))
    grads = pullback(cotangent.astype(jnp.float32))
    return (output.astype(jnp.bfloat16), grads[0], grads[1], grads[2], grads[3], grads[4], grads[5], grads[6], grads[7], grads[8], grads[9], grads[10], grads[11], grads[12], grads[13])
```

```python
import jax
import jax.numpy as jnp
from jax import lax
from jax.sharding import PartitionSpec as P
from jax.experimental import pallas as pl
from jax.experimental.pallas import tpu as pltpu

FSDP = "fsdp"
HEADS = "heads"
TENSOR = "tensor"
SCORE = "qhd,khd->hqk"
MIX = "hqk,khd->qhd"
BACK = "hqk,qhd->khd"

D = 2048
NOPE = 128
ROPE = 64
VDIM = 128
KVR = 512
TOP = 6
EXP_LOC = 2
LEN = 512
SEQ_DEV = 1


epsilon = 1e-06
theta_base = 10000.0


def rms_parts(vector):
    inverse = lax.rsqrt(jnp.mean(vector * vector, axis=-1, keepdims=True) + epsilon)
    return (vector * inverse, inverse)


def rms_back(grad_norm, normed, inverse, gain_vec):
    scaled = grad_norm * gain_vec
    inner_mean = jnp.mean(scaled * normed, axis=-1, keepdims=True)
    return inverse * (scaled - normed * inner_mean)


def rope_tables(row_count):
    half_width = ROPE // 2
    position = (jnp.arange(row_count) % LEN).astype(jnp.float32)
    exponent = jnp.arange(half_width).astype(jnp.float32) * (2.0 / ROPE)
    frequency = theta_base ** (-exponent)
    angles = position[:, None] * frequency[None, :]
    return (jnp.cos(angles), jnp.sin(angles))


def rotate(vector, cosine, sine_table):
    half_width = vector.shape[-1] // 2
    first_half = vector[..., :half_width]
    second_half = vector[..., half_width:]
    return jnp.concatenate(
        [
            first_half * cosine - second_half * sine_table,
            second_half * cosine + first_half * sine_table,
        ],
        axis=-1,
    )


def unrotate(vector, cosine, sine_table):
    half_width = vector.shape[-1] // 2
    first_half = vector[..., :half_width]
    second_half = vector[..., half_width:]
    return jnp.concatenate(
        [
            first_half * cosine + second_half * sine_table,
            second_half * cosine - first_half * sine_table,
        ],
        axis=-1,
    )


def combine(returned, positions, weighting, block_rows):
    width = returned.shape[-1]
    padded = jnp.concatenate(
        [returned.reshape(-1, width), jnp.zeros((1, width), jnp.float32)], axis=0
    )
    summed = jnp.zeros((block_rows, width), jnp.float32)
    for route_index in range(TOP):
        picked = padded[positions[:, route_index]]
        if weighting is None:
            summed = summed + picked
        else:
            summed = summed + picked * weighting[:, route_index : route_index + 1]
    return summed


def dispatch(outgoing):
    return lax.all_to_all(outgoing, (FSDP, HEADS), split_axis=0, concat_axis=0, tiled=True)


def bring_back(host_term, local_term, positions, weighting):
    block_rows = local_term.shape[0]
    arrived_rows = lax.all_to_all(
        host_term.astype(jnp.bfloat16), (FSDP, HEADS), split_axis=0, concat_axis=0, tiled=True
    ).astype(host_term.dtype)
    merged = combine(arrived_rows, positions, weighting, block_rows) + local_term
    own_rows = lax.psum_scatter(
        merged.astype(jnp.bfloat16), TENSOR, scatter_dimension=0, tiled=True
    ).astype(jnp.float32)
    return (
        own_rows,
        lax.all_gather(own_rows.astype(jnp.bfloat16), HEADS, axis=0, tiled=True).astype(
            own_rows.dtype
        ),
    )


def shards(
    block_input,
    cotangent,
    norm1_gain,
    latent_gain,
    norm2_gain,
    w_query,
    w_latent,
    w_kv,
    w_out,
    expert_gate,
    expert_up,
    expert_down,
    shared_gate,
    shared_up,
    shared_down,
    routed_expert_index,
    slots,
    gate_weights,
):
    row_count = block_input.shape[0]
    head_dim = NOPE + ROPE
    local_heads = w_query.shape[1] // head_dim
    score_scale = head_dim ** (-0.5)
    query_full, latent_full, kv_full, out_full = (
        lax.all_gather(w_query, (FSDP, TENSOR), axis=0, tiled=True),
        lax.all_gather(w_latent, (FSDP, TENSOR), axis=0, tiled=True),
        lax.all_gather(w_kv, (FSDP, TENSOR), axis=0, tiled=True),
        lax.all_gather(w_out, (FSDP, TENSOR), axis=1, tiled=True),
    )
    shared_gate_full, shared_up_full, shared_down_full = (
        lax.all_gather(shared_gate, (FSDP, HEADS), axis=0, tiled=True),
        lax.all_gather(shared_up, (FSDP, HEADS), axis=0, tiled=True),
        lax.all_gather(shared_down, (FSDP, HEADS), axis=1, tiled=True),
    )
    residual = block_input.astype(jnp.float32)
    first_normed, first_inverse = rms_parts(residual)
    first_input = (first_normed * norm1_gain).astype(jnp.bfloat16)
    cosine, sine_table = rope_tables(row_count)
    query_raw = jnp.dot(first_input, query_full, preferred_element_type=jnp.float32).reshape(
        row_count, local_heads, head_dim
    )
    queries = jnp.concatenate(
        [
            query_raw[..., :NOPE],
            rotate(query_raw[..., NOPE:], cosine[:, None, :], sine_table[:, None, :]),
        ],
        axis=-1,
    ).astype(jnp.bfloat16)
    latent_raw = jnp.dot(first_input, latent_full, preferred_element_type=jnp.float32)
    latent_normed, latent_inverse = rms_parts(latent_raw[:, :KVR])
    latent_norm = (latent_normed * latent_gain).astype(jnp.bfloat16)
    key_rope = rotate(latent_raw[:, KVR:], cosine, sine_table).astype(jnp.bfloat16)
    key_value = (
        jnp.dot(latent_norm, kv_full, preferred_element_type=jnp.float32)
        .astype(jnp.bfloat16)
        .reshape(row_count, local_heads, NOPE + VDIM)
    )
    key_all = jnp.concatenate(
        [
            key_value[..., :NOPE],
            jnp.broadcast_to(key_rope[:, None, :], (row_count, local_heads, ROPE)),
        ],
        axis=-1,
    )
    values = key_value[..., NOPE:]
    causal = jnp.arange(LEN)[:, None] >= jnp.arange(LEN)[None, :]

    def score_block(queries_s, keys_s):
        scores = (
            jnp.einsum(SCORE, queries_s, keys_s, preferred_element_type=jnp.float32)
            * score_scale
        )
        return jnp.where(causal[None], scores, -1e30)

    def attend(pieces):
        queries_s, keys_s, values_s = pieces
        scores = score_block(queries_s, keys_s)
        highest_score = jnp.max(scores, axis=-1, keepdims=True)
        log_total = highest_score + jnp.log(
            jnp.sum(jnp.exp(scores - highest_score), axis=-1, keepdims=True)
        )
        probabilities = jnp.exp(scores - log_total).astype(jnp.bfloat16)
        context_s = jnp.einsum(
            MIX, probabilities, values_s, preferred_element_type=jnp.float32
        )
        return (context_s.astype(jnp.bfloat16), log_total)

    seq_queries = queries.reshape(SEQ_DEV, LEN, local_heads, head_dim)
    seq_keys = key_all.reshape(SEQ_DEV, LEN, local_heads, head_dim)
    seq_values = values.reshape(SEQ_DEV, LEN, local_heads, VDIM)
    context, log_totals = lax.map(attend, (seq_queries, seq_keys, seq_values))
    context_flat = context.reshape(row_count, local_heads * VDIM)
    attention_part = jnp.dot(context_flat, out_full, preferred_element_type=jnp.float32)
    after_attention = residual + lax.psum(attention_part.astype(jnp.bfloat16), HEADS).astype(
        jnp.float32
    )
    second_normed, second_inverse = rms_parts(after_attention)
    second_input = (second_normed * norm2_gain).astype(jnp.bfloat16)
    quarter = row_count // lax.axis_size(HEADS)
    row_start = lax.axis_index(HEADS) * quarter

    def own_part(array):
        return lax.dynamic_slice_in_dim(array, row_start, quarter, 0)

    tokens_in, grads_in, ids_in, slots_in, gates_in = (
        lax.all_gather(own_part(second_input), TENSOR, axis=0, tiled=True),
        lax.all_gather(own_part(cotangent), TENSOR, axis=0, tiled=True),
        lax.all_gather(own_part(routed_expert_index), TENSOR, axis=0, tiled=True),
        lax.all_gather(own_part(slots), TENSOR, axis=0, tiled=True),
        lax.all_gather(own_part(gate_weights), TENSOR, axis=0, tiled=True),
    )
    hosts = lax.axis_size(FSDP) * lax.axis_size(HEADS)
    experts = EXP_LOC * hosts
    block_rows = tokens_in.shape[0]
    capacity = block_rows * TOP * 5 // (4 * experts)
    positions = jnp.where(slots_in < capacity, ids_in * capacity + slots_in, experts * capacity)
    flat_positions = positions.reshape(-1)
    row_labels = jnp.repeat(jnp.arange(block_rows, dtype=jnp.int32), TOP)
    owners = (
        jnp.full((experts * capacity + 1,), block_rows, jnp.int32)
        .at[flat_positions]
        .set(row_labels)[: experts * capacity]
    )
    routing_gate_weights = gates_in.astype(jnp.float32)
    slot_gates = (
        jnp.zeros((experts * capacity + 1,), jnp.float32)
        .at[flat_positions]
        .set(routing_gate_weights.reshape(-1))[: experts * capacity]
    )
    buffer_shape = (hosts, EXP_LOC, capacity, D)
    tokens_padded = jnp.concatenate([tokens_in, jnp.zeros((1, D), jnp.bfloat16)], axis=0)
    arrived = dispatch(tokens_padded[owners].reshape(buffer_shape))
    gate_act = jnp.einsum(
        "secd,edf->secf", arrived, expert_gate, preferred_element_type=jnp.float32
    )
    up_act = jnp.einsum("secd,edf->secf", arrived, expert_up, preferred_element_type=jnp.float32)
    gate_sigmoid = jax.nn.sigmoid(gate_act)
    gate_silu = gate_act * gate_sigmoid
    expert_hidden = (gate_silu * up_act).astype(jnp.bfloat16)
    expert_out = jnp.einsum(
        "secf,efd->secd", expert_hidden, expert_down, preferred_element_type=jnp.float32
    )
    shared_act = jnp.dot(tokens_in, shared_gate_full, preferred_element_type=jnp.float32)
    shared_lin = jnp.dot(tokens_in, shared_up_full, preferred_element_type=jnp.float32)
    shared_sigmoid = jax.nn.sigmoid(shared_act)
    shared_silu = shared_act * shared_sigmoid
    shared_hidden = (shared_silu * shared_lin).astype(jnp.bfloat16)
    shared_out = jnp.dot(shared_hidden, shared_down_full, preferred_element_type=jnp.float32)
    ffn_rows, ffn_full = bring_back(expert_out, shared_out, positions, routing_gate_weights)
    output = (after_attention + ffn_full).astype(jnp.bfloat16)
    grads_padded = jnp.concatenate([grads_in, jnp.zeros((1, D), jnp.bfloat16)], axis=0)
    grad_slots = (
        (grads_padded[owners].astype(jnp.float32) * slot_gates[:, None])
        .astype(jnp.bfloat16)
        .reshape(buffer_shape)
    )
    grad_arrived = dispatch(grad_slots)
    grad_hidden = jnp.einsum(
        "secd,efd->secf", grad_arrived, expert_down, preferred_element_type=jnp.float32
    )
    grad_gate = (
        grad_hidden * up_act * gate_sigmoid * (1.0 + gate_act * (1.0 - gate_sigmoid))
    ).astype(jnp.bfloat16)
    grad_up = (grad_hidden * gate_silu).astype(jnp.bfloat16)
    expert_down_grad = jnp.einsum(
        "secf,secd->efd", expert_hidden, grad_arrived, preferred_element_type=jnp.float32
    )
    expert_gate_grad = jnp.einsum(
        "secd,secf->edf", arrived, grad_gate, preferred_element_type=jnp.float32
    )
    expert_up_grad = jnp.einsum(
        "secd,secf->edf", arrived, grad_up, preferred_element_type=jnp.float32
    )
    host_back = jnp.einsum(
        "secf,edf->secd", grad_gate, expert_gate, preferred_element_type=jnp.float32
    ) + jnp.einsum("secf,edf->secd", grad_up, expert_up, preferred_element_type=jnp.float32)
    grad_shared_hidden = jnp.dot(grads_in, shared_down_full.T, preferred_element_type=jnp.float32)
    shared_gate_back = (
        grad_shared_hidden
        * shared_lin
        * shared_sigmoid
        * (1.0 + shared_act * (1.0 - shared_sigmoid))
    ).astype(jnp.bfloat16)
    shared_up_back = (grad_shared_hidden * shared_silu).astype(jnp.bfloat16)
    shared_down_part = jnp.dot(shared_hidden.T, grads_in, preferred_element_type=jnp.float32)
    shared_gate_part = jnp.dot(tokens_in.T, shared_gate_back, preferred_element_type=jnp.float32)
    shared_up_part = jnp.dot(tokens_in.T, shared_up_back, preferred_element_type=jnp.float32)
    shared_gate_grad, shared_up_grad, shared_down_grad = (
        lax.psum_scatter(
            shared_gate_part.astype(jnp.bfloat16),
            (FSDP, HEADS),
            scatter_dimension=0,
            tiled=True,
        ).astype(jnp.float32),
        lax.psum_scatter(
            shared_up_part.astype(jnp.bfloat16), (FSDP, HEADS), scatter_dimension=0, tiled=True
        ).astype(jnp.float32),
        lax.psum_scatter(
            shared_down_part.astype(jnp.bfloat16),
            (FSDP, HEADS),
            scatter_dimension=1,
            tiled=True,
        ).astype(jnp.float32),
    )
    shared_back = jnp.dot(
        shared_gate_back, shared_gate_full.T, preferred_element_type=jnp.float32
    ) + jnp.dot(shared_up_back, shared_up_full.T, preferred_element_type=jnp.float32)
    grad_rows, grad_second = bring_back(host_back, shared_back, positions, None)
    second_gain_part = jnp.sum(grad_second * second_normed, axis=0)
    grad_after = cotangent.astype(jnp.float32) + rms_back(
        grad_second, second_normed, second_inverse, norm2_gain
    )
    grad_attention = grad_after.astype(jnp.bfloat16)
    out_part = jnp.dot(context_flat.T, grad_attention, preferred_element_type=jnp.float32)
    grad_context = (
        jnp.dot(grad_attention, out_full.T, preferred_element_type=jnp.float32)
        .astype(jnp.bfloat16)
        .reshape(SEQ_DEV, LEN, local_heads, VDIM)
    )

    def attend_back(pieces):
        queries_s, keys_s, values_s, log_total, grad_context_s = pieces
        scores = score_block(queries_s, keys_s)
        probabilities = jnp.exp(scores - log_total)
        grad_probs = jnp.einsum(
            SCORE, grad_context_s, values_s, preferred_element_type=jnp.float32
        )
        centred = jnp.sum(probabilities * grad_probs, axis=-1, keepdims=True)
        grad_scores = (probabilities * (grad_probs - centred)).astype(jnp.bfloat16)
        grad_queries_s = (
            jnp.einsum(MIX, grad_scores, keys_s, preferred_element_type=jnp.float32)
            * score_scale
        )
        grad_keys_s = (
            jnp.einsum(BACK, grad_scores, queries_s, preferred_element_type=jnp.float32)
            * score_scale
        )
        grad_values_s = jnp.einsum(
            BACK,
            probabilities.astype(jnp.bfloat16),
            grad_context_s,
            preferred_element_type=jnp.float32,
        )
        return (grad_queries_s, grad_keys_s, grad_values_s)

    grad_queries, grad_keys, grad_values = lax.map(
        attend_back, (seq_queries, seq_keys, seq_values, log_totals, grad_context)
    )
    grad_queries = grad_queries.reshape(row_count, local_heads, head_dim)
    grad_keys = grad_keys.reshape(row_count, local_heads, head_dim)
    grad_values = grad_values.reshape(row_count, local_heads, VDIM)
    grad_query_raw = (
        jnp.concatenate(
            [
                grad_queries[..., :NOPE],
                unrotate(grad_queries[..., NOPE:], cosine[:, None, :], sine_table[:, None, :]),
            ],
            axis=-1,
        )
        .astype(jnp.bfloat16)
        .reshape(row_count, local_heads * head_dim)
    )
    query_part = jnp.dot(first_input.T, grad_query_raw, preferred_element_type=jnp.float32)
    first_from_query = jnp.dot(grad_query_raw, query_full.T, preferred_element_type=jnp.float32)
    grad_key_value = (
        jnp.concatenate([grad_keys[..., :NOPE], grad_values], axis=-1)
        .astype(jnp.bfloat16)
        .reshape(row_count, local_heads * (NOPE + VDIM))
    )
    kv_part = jnp.dot(latent_norm.T, grad_key_value, preferred_element_type=jnp.float32)
    grad_latent_norm = jnp.dot(grad_key_value, kv_full.T, preferred_element_type=jnp.float32)
    latent_gain_part = jnp.sum(grad_latent_norm * latent_normed, axis=0)
    grad_compressed = rms_back(grad_latent_norm, latent_normed, latent_inverse, latent_gain)
    grad_key_rope = unrotate(jnp.sum(grad_keys[..., NOPE:], axis=1), cosine, sine_table)
    latent_term = jnp.concatenate([grad_compressed, grad_key_rope], axis=-1)
    first_summed, latent_summed, latent_gain_summed = (
        lax.psum(first_from_query.astype(jnp.bfloat16), HEADS).astype(jnp.float32),
        lax.psum(latent_term.astype(jnp.bfloat16), HEADS).astype(jnp.float32),
        lax.psum(latent_gain_part.astype(jnp.bfloat16), HEADS).astype(jnp.float32),
    )
    grad_latent = latent_summed.astype(jnp.bfloat16)
    latent_part = jnp.dot(first_input.T, grad_latent, preferred_element_type=jnp.float32)
    grad_first = first_summed + jnp.dot(
        grad_latent, latent_full.T, preferred_element_type=jnp.float32
    )
    first_gain_part = jnp.sum(grad_first * first_normed, axis=0)
    input_grad = grad_after + rms_back(grad_first, first_normed, first_inverse, norm1_gain)
    (
        w_query_grad,
        w_latent_grad,
        w_kv_grad,
        w_out_grad,
        norm1_gain_grad,
        latent_gain_grad,
        norm2_gain_grad,
    ) = (
        lax.psum_scatter(
            query_part.astype(jnp.bfloat16), (FSDP, TENSOR), scatter_dimension=0, tiled=True
        ).astype(jnp.float32),
        lax.psum_scatter(
            latent_part.astype(jnp.bfloat16), (FSDP, TENSOR), scatter_dimension=0, tiled=True
        ).astype(jnp.float32),
        lax.psum_scatter(
            kv_part.astype(jnp.bfloat16), (FSDP, TENSOR), scatter_dimension=0, tiled=True
        ).astype(jnp.float32),
        lax.psum_scatter(
            out_part.astype(jnp.bfloat16), (FSDP, TENSOR), scatter_dimension=1, tiled=True
        ).astype(jnp.float32),
        lax.psum_scatter(
            first_gain_part.astype(jnp.bfloat16),
            (FSDP, TENSOR),
            scatter_dimension=0,
            tiled=True,
        ).astype(jnp.float32),
        lax.psum_scatter(
            latent_gain_summed.astype(jnp.bfloat16),
            (FSDP, TENSOR),
            scatter_dimension=0,
            tiled=True,
        ).astype(jnp.float32),
        lax.psum_scatter(
            second_gain_part.astype(jnp.bfloat16),
            (FSDP, TENSOR),
            scatter_dimension=0,
            tiled=True,
        ).astype(jnp.float32),
    )
    return (
        output,
        input_grad,
        norm1_gain_grad,
        latent_gain_grad,
        norm2_gain_grad,
        w_query_grad,
        w_latent_grad,
        w_kv_grad,
        w_out_grad,
        expert_gate_grad,
        expert_up_grad,
        expert_down_grad,
        shared_gate_grad,
        shared_up_grad,
        shared_down_grad,
    )


PLANE = (FSDP, HEADS)
GROUPS = ((0,), (1, 3), (2,))
LANES = 128
TILE = 256
bf16 = jnp.bfloat16
f32 = jnp.float32


def after(array, *others):
    return lax.optimization_barrier((array, *others))[0]


def from_tensor(array, k):
    return lax.ppermute(array, TENSOR, [((i + k) % 4, i) for i in range(4)])


def to_tensor(array, k):
    return lax.ppermute(array, TENSOR, [(i, (i + k) % 4) for i in range(4)])


def swap_fsdp(array):
    return lax.ppermute(array, FSDP, [(0, 1), (1, 0)])


def swap_heads(array, mask):
    return lax.ppermute(array, HEADS, [(i, i ^ mask) for i in range(4)])


def swap_plane(array, first):
    pairs = []
    for f in range(2):
        for h in range(4):
            f_to, h_to = (f ^ 1, h) if h % 2 == first else (f, h ^ 2)
            pairs.append((f * 4 + h, f_to * 4 + h_to))
    return lax.ppermute(array, PLANE, pairs)


def gather_rows(unit):
    along = {0: unit}
    for k in (1, 3, 2):
        along[k] = from_tensor(unit, k)
    groups = []
    for group in GROUPS:
        mine = jnp.concatenate([along[k] for k in group], axis=0)
        mine = jnp.concatenate([mine, swap_plane(mine, 0)], axis=0)
        mine = jnp.concatenate([mine, swap_plane(mine, 1)], axis=0)
        groups.append((mine, swap_heads(mine, 1)))
    return groups


def scatter_rows(groups):
    total = None
    for group, (mine, other) in zip(GROUPS, groups):
        other = swap_heads(other, 1)
        half = mine.shape[0] // 2
        sent = swap_plane((mine[half:].astype(f32) + other[half:].astype(f32)).astype(bf16), 1)
        part = half // 2
        near = [a[:part].astype(f32) for a in (mine, other, sent)]
        far = [a[part:half].astype(f32) for a in (mine, other)] + [sent[part:].astype(f32)]
        far = swap_plane((far[0] + far[1] + far[2]).astype(bf16), 0)
        summed = near[0] + near[1] + near[2] + far.astype(f32)
        for k, piece in zip(group, jnp.split(summed, len(group), axis=0)):
            if k:
                piece = to_tensor(piece.astype(bf16), k).astype(f32)
            total = piece if total is None else total + piece
    return total


def gather_weight(shard, *before_swap):
    along = {0: shard}
    for k in (1, 3, 2):
        along[k] = from_tensor(shard, k)
    along = [along[k] for k in range(4)]
    return along + [swap_fsdp(after(p, *before_swap) if before_swap else p) for p in along]


def scatter_weight(parts):
    near, far = parts[:4], swap_fsdp(parts[4:].astype(bf16))
    summed = near.astype(f32) + far.astype(f32)
    total = summed[0]
    for k in (1, 3, 2):
        total = total + to_tensor(summed[k].astype(bf16), k).astype(f32)
    return total


def pick(array, index, count, axis):
    size = array.shape[axis] // count
    return lax.dynamic_slice_in_dim(array, index * size, size, axis)


def nn(left, right):
    return jnp.dot(left, right, preferred_element_type=f32)


def nt(left, right):
    return lax.dot_general(left, right, (((1,), (1,)), ((), ())), preferred_element_type=f32)


def hidden_kernel(
    first_ref,
    x1_ref,
    x2_ref,
    g1_ref,
    g2_ref,
    r1_ref,
    r2_ref,
    gate_ref,
    up_ref,
    down_ref,
    d1_ref,
    d2_ref,
    h_ref,
    bg_ref,
    bu_ref,
    x_scr,
    g_scr,
    r_scr,
):
    step = pl.program_id(0)
    half = pl.num_programs(0) // 2
    for near, x_ref, g_ref, r_ref in (
        (True, x1_ref, g1_ref, r1_ref),
        (False, x2_ref, g2_ref, r2_ref),
    ):

        @pl.when((step < half) == near)
        def _(x_ref=x_ref, g_ref=g_ref, r_ref=r_ref):
            x_scr[...] = x_ref[...]
            g_scr[...] = g_ref[...]
            r_scr[...] = r_ref[...]

    rows = x_scr[...]
    routes = r_scr[...].astype(f32)
    width = gate_ref.shape[1]
    part = (width - LANES) // EXP_LOC
    lane = lax.broadcasted_iota(jnp.int32, routes.shape, 1)
    scales = [
        jnp.sum(jnp.where(lane == first_ref[0] + e, routes, 0.0), axis=1, keepdims=True)
        for e in range(EXP_LOC)
    ]
    column = lax.broadcasted_iota(jnp.int32, (1, width), 1)
    scale = jnp.where(
        column < part, scales[0], jnp.where(column < EXP_LOC * part, scales[1], 1.0)
    )
    gate_act = nn(rows, gate_ref[...])
    up_act = nn(rows, up_ref[...])
    sigmoid = jax.nn.sigmoid(gate_act)
    silu = gate_act * sigmoid
    h_ref[...] = (silu * up_act * scale).astype(bf16)
    grad_hidden = nt(g_scr[...], down_ref[...]) * scale
    back_gate = (grad_hidden * up_act * (sigmoid + silu * (1.0 - sigmoid))).astype(bf16)
    back_up = (grad_hidden * silu).astype(bf16)
    bg_ref[...] = back_gate
    bu_ref[...] = back_up
    result = (nt(back_gate, gate_ref[...]) + nt(back_up, up_ref[...])).astype(bf16)

    @pl.when(step < half)
    def _():
        d1_ref[...] = result

    @pl.when(step >= half)
    def _():
        d2_ref[...] = result


def hidden_step(first, rows, grads, gate_all, up_all, down_all):
    count = rows[0].shape[0]
    half = count // TILE
    width = gate_all.shape[1]

    def near(i, first):
        return (jnp.minimum(i, half - 1), 0)

    def far(i, first):
        return (jnp.maximum(i - half, 0), 0)

    def near_routes(i, first):
        return (jnp.minimum(i, half - 1), D // LANES)

    def far_routes(i, first):
        return (jnp.maximum(i - half, 0), D // LANES)

    def whole(i, first):
        return (0, 0)

    def step(i, first):
        return (i, 0)

    once = pl.Buffered(1)
    row_shape = jax.ShapeDtypeStruct((count, D), bf16)
    hidden_shape = jax.ShapeDtypeStruct((2 * count, width), bf16)
    return pl.pallas_call(
        hidden_kernel,
        out_shape=(row_shape, row_shape, hidden_shape, hidden_shape, hidden_shape),
        grid_spec=pltpu.PrefetchScalarGridSpec(
            num_scalar_prefetch=1,
            grid=(2 * half,),
            in_specs=[
                pl.BlockSpec((TILE, D), near),
                pl.BlockSpec((TILE, D), far),
                pl.BlockSpec((TILE, D), near),
                pl.BlockSpec((TILE, D), far),
                pl.BlockSpec((TILE, LANES), near_routes),
                pl.BlockSpec((TILE, LANES), far_routes),
                pl.BlockSpec((D, width), whole, pipeline_mode=once),
                pl.BlockSpec((D, width), whole, pipeline_mode=once),
                pl.BlockSpec((width, D), whole, pipeline_mode=once),
            ],
            out_specs=[
                pl.BlockSpec((TILE, D), near),
                pl.BlockSpec((TILE, D), far),
                pl.BlockSpec((TILE, width), step),
                pl.BlockSpec((TILE, width), step),
                pl.BlockSpec((TILE, width), step),
            ],
            scratch_shapes=[
                pltpu.VMEM((TILE, D), bf16),
                pltpu.VMEM((TILE, D), bf16),
                pltpu.VMEM((TILE, LANES), bf16),
            ],
        ),
        compiler_params=pltpu.CompilerParams(vmem_limit_bytes=60000 * 1024),
        cost_estimate=pl.CostEstimate(
            flops=2 * count * D * width * 10,
            bytes_accessed=2 * count * (3 * D + 3 * width) * 2 + 3 * D * width * 2,
            transcendentals=2 * count * width,
        ),
    )(first, rows[0], rows[1], grads[0], grads[1], grads[0], grads[1], gate_all, up_all, down_all)


def dense_shards(
    block_input,
    cotangent,
    norm1_gain,
    latent_gain,
    norm2_gain,
    w_query,
    w_latent,
    w_kv,
    w_out,
    expert_gate,
    expert_up,
    expert_down,
    shared_gate,
    shared_up,
    shared_down,
    routed_expert_index,
    slots,
    gate_weights,
):
    f = lax.axis_index(FSDP)
    h = lax.axis_index(HEADS)
    t = lax.axis_index(TENSOR)
    row_count = block_input.shape[0]
    head_dim = NOPE + ROPE
    local_heads = w_query.shape[1] // head_dim
    query_width = local_heads * head_dim
    score_scale = head_dim ** (-0.5)
    hosts = lax.axis_size(FSDP) * lax.axis_size(HEADS)
    experts = EXP_LOC * hosts
    capacity = row_count * TOP * 5 // (4 * experts)

    relative = [(f ^ dx) * 4 + (t + k) % 4 for dx in range(2) for k in range(4)]
    absolute = [(F ^ f) * 4 + (T - t) % 4 for F in range(2) for T in range(4)]
    turns = (0, 2, 1, 3)

    def chunks_to(array, order, axis):
        return jnp.concatenate([pick(array, i, 8, axis) for i in order], axis=axis)

    def quarter(array):
        return pick(array, h, 4, 0)

    def rows_relative(array):
        return jnp.concatenate([pick(array, h ^ j, 4, 0) for j in turns], axis=0)

    def rows_absolute(array):
        places = [h ^ i for i in range(4)]
        return jnp.concatenate([pick(array, (p % 2) * 2 + p // 2, 4, 0) for p in places], axis=0)

    def reduce_heads(partial):
        half = partial.shape[0] // 2
        summed = partial[:half] + swap_heads(partial[half:].astype(bf16), 1).astype(f32)
        half //= 2
        return summed[:half] + swap_heads(summed[half:].astype(bf16), 2).astype(f32)

    def gather_heads(own):
        near = jnp.concatenate([own, swap_heads(own, 2)], axis=0)
        return jnp.concatenate([near, swap_heads(near, 1)], axis=0)

    kv_rows = w_kv.shape[0]
    kv_width = w_kv.shape[0] * w_kv.shape[1] // w_query.shape[0]
    latent_width = w_latent.shape[1] // 4
    kv_start = query_width + latent_width
    first_pack = jnp.concatenate(
        [w_query, pick(w_latent, h, 4, 1), w_kv.reshape(-1, kv_width)], axis=1
    )
    first_parts = gather_weight(first_pack)
    w_first = jnp.concatenate(first_parts, axis=0)
    w_queries, w_latents = w_first[:, :query_width], w_first[:, query_width:kv_start]
    kv_full = jnp.concatenate([p[:, kv_start:].reshape(kv_rows, -1) for p in first_parts], axis=0)
    kv_full = chunks_to(kv_full, absolute, 0)

    own_ids, own_slots, own_gates = quarter(routed_expert_index), quarter(slots), quarter(gate_weights)
    lanes = jnp.arange(LANES)[None, None, :]
    used_route = (own_ids[:, :, None] == lanes) & (own_slots[:, :, None] < capacity)
    route_weights = jnp.sum(jnp.where(used_route, own_gates[:, :, None].astype(f32), 0.0), axis=1)
    cotangent_own = quarter(cotangent)
    grad_unit = jnp.concatenate([cotangent_own, route_weights.astype(bf16)], axis=1)

    shared_two = lax.all_to_all(
        jnp.stack([shared_gate, shared_up]), PLANE, split_axis=2, concat_axis=1, tiled=True
    )
    shared_down_own = lax.all_to_all(shared_down, PLANE, split_axis=0, concat_axis=1, tiled=True)
    hidden = expert_gate.shape[2]
    part = -(-hidden // LANES) * LANES
    shared_hidden = shared_two.shape[2]
    width = EXP_LOC * part + LANES

    def side_by_side(routed, shared, axis):
        pieces = []
        for piece in [routed[e] for e in range(EXP_LOC)] + [shared]:
            fill = -piece.shape[axis] % LANES
            pieces.append(jnp.pad(piece, [(0, fill if a == axis else 0) for a in range(2)]))
        return jnp.concatenate(pieces, axis=axis)

    gate_all = side_by_side(expert_gate, shared_two[0], 1)
    up_all = side_by_side(expert_up, shared_two[1], 1)
    down_all = side_by_side(expert_down, shared_down_own, 0)

    residual = chunks_to(block_input, relative, 1).astype(f32)
    gain1 = chunks_to(norm1_gain, relative, 0)
    first_normed, first_inverse = rms_parts(residual)
    first_input = (first_normed * gain1).astype(bf16)
    cosine, sine_table = rope_tables(row_count)
    first_input = after(first_input, gate_all, up_all, down_all)
    latent_own = lax.dot_general(
        w_latents, first_input, (((0,), (1,)), ((), ())), preferred_element_type=f32
    )
    latent_raw = rows_absolute(gather_heads(latent_own.astype(bf16))).T.astype(f32)
    query_raw = nn(first_input, w_queries).reshape(row_count, local_heads, head_dim)
    out_parts = gather_weight(after(w_out, *first_parts[1:4]), query_raw)
    out_full = jnp.concatenate(out_parts, axis=1)
    queries = jnp.concatenate(
        [
            query_raw[..., :NOPE],
            rotate(query_raw[..., NOPE:], cosine[:, None, :], sine_table[:, None, :]),
        ],
        axis=-1,
    ).astype(bf16)
    latent_normed, latent_inverse = rms_parts(latent_raw[:, :KVR])
    latent_norm = (latent_normed * latent_gain).astype(bf16)
    key_rope = rotate(latent_raw[:, KVR:], cosine, sine_table).astype(bf16)
    key_value = nn(latent_norm, kv_full).astype(bf16).reshape(row_count, local_heads, NOPE + VDIM)
    keys = jnp.concatenate(
        [
            key_value[..., :NOPE],
            jnp.broadcast_to(key_rope[:, None, :], (row_count, local_heads, ROPE)),
        ],
        axis=-1,
    )
    values = key_value[..., NOPE:]
    grads = gather_rows(after(grad_unit, key_value))
    causal = jnp.arange(LEN)[:, None] >= jnp.arange(LEN)[None, :]

    def score_block():
        scores = jnp.einsum(SCORE, queries, keys, preferred_element_type=f32) * score_scale
        return jnp.where(causal[None], scores, -1e30)

    scores = score_block()
    highest_score = jnp.max(scores, axis=-1, keepdims=True)
    log_total = highest_score + jnp.log(
        jnp.sum(jnp.exp(scores - highest_score), axis=-1, keepdims=True)
    )
    probabilities = jnp.exp(scores - log_total).astype(bf16)
    context = jnp.einsum(MIX, probabilities, values, preferred_element_type=f32)
    context = rows_relative(context.astype(bf16).reshape(row_count, local_heads * VDIM))
    attention_own = reduce_heads(nn(context, out_full))
    after_attention = quarter(block_input).astype(f32) + chunks_to(attention_own, absolute, 1)
    second_normed, second_inverse = rms_parts(after_attention)
    second_input = (second_normed * norm2_gain).astype(bf16)

    rows = gather_rows(second_input)
    first_expert = ((f * lax.axis_size(HEADS) + h) * EXP_LOC).astype(jnp.int32).reshape(1)
    grad_groups, hidden_parts, gate_parts, up_parts = [], [], [], []
    for rows_g, grads_g in zip(rows, grads):
        near, far, hidden_g, gate_g, up_g = hidden_step(
            first_expert, rows_g, grads_g, gate_all, up_all, down_all
        )
        grad_groups.append((near, far))
        hidden_parts.append(hidden_g)
        gate_parts.append(gate_g)
        up_parts.append(up_g)
    grad_second = scatter_rows(grad_groups)

    second_gain_part = jnp.sum(grad_second * second_normed, axis=0)
    grad_after = cotangent_own.astype(f32) + rms_back(
        grad_second, second_normed, second_inverse, norm2_gain
    )
    grad_after = chunks_to(grad_after, relative, 1)
    grad_attention = gather_heads(grad_after.astype(bf16))
    out_part = nn(context.T, grad_attention)
    grad_context = nt(grad_attention, out_full).astype(bf16)
    grad_context = rows_absolute(grad_context).reshape(row_count, local_heads, VDIM)
    probabilities = jnp.exp(score_block() - log_total)
    grad_probs = jnp.einsum(SCORE, grad_context, values, preferred_element_type=f32)
    centred = jnp.sum(probabilities * grad_probs, axis=-1, keepdims=True)
    grad_scores = (probabilities * (grad_probs - centred)).astype(bf16)
    grad_queries = (
        jnp.einsum(MIX, grad_scores, keys, preferred_element_type=f32) * score_scale
    )
    grad_keys = (
        jnp.einsum(BACK, grad_scores, queries, preferred_element_type=f32) * score_scale
    )
    grad_values = jnp.einsum(
        BACK, probabilities.astype(bf16), grad_context, preferred_element_type=f32
    )
    grad_query_raw = (
        jnp.concatenate(
            [
                grad_queries[..., :NOPE],
                unrotate(grad_queries[..., NOPE:], cosine[:, None, :], sine_table[:, None, :]),
            ],
            axis=-1,
        )
        .astype(bf16)
        .reshape(row_count, query_width)
    )
    first_from_query = nt(rows_relative(grad_query_raw), w_queries)
    grad_key_value = (
        jnp.concatenate([grad_keys[..., :NOPE], grad_values], axis=-1)
        .astype(bf16)
        .reshape(row_count, local_heads * (NOPE + VDIM))
    )
    grad_latent_norm = nt(grad_key_value, kv_full)
    latent_gain_part = jnp.sum(grad_latent_norm * latent_normed, axis=0)
    grad_compressed = rms_back(grad_latent_norm, latent_normed, latent_inverse, latent_gain)
    grad_key_rope = unrotate(jnp.sum(grad_keys[..., NOPE:], axis=1), cosine, sine_table)
    latent_term = jnp.concatenate([grad_compressed, grad_key_rope], axis=-1)
    grad_latent = reduce_heads(rows_relative(latent_term.T)).astype(bf16)
    grad_latent_rows = jnp.concatenate([pick(grad_latent, h ^ j, 4, 1) for j in turns], axis=1)
    first_from_latent = lax.dot_general(
        grad_latent_rows, w_latents, (((0,), (1,)), ((), ())), preferred_element_type=f32
    )
    query_part = nn(first_input.T, grad_query_raw)
    kv_part = nn(latent_norm.T, grad_key_value)
    latent_part = lax.dot_general(
        first_input, grad_latent, (((0,), (1,)), ((), ())), preferred_element_type=f32
    )
    grad_first = reduce_heads(first_from_query + first_from_latent)
    first_normed_own = quarter(first_normed)
    first_gain_part = jnp.sum(grad_first * first_normed_own, axis=0)
    input_own = grad_after + rms_back(grad_first, first_normed_own, quarter(first_inverse), gain1)
    input_grad = rows_absolute(gather_heads(chunks_to(input_own.astype(bf16), absolute, 1))).astype(f32)

    out_pieces = jnp.stack([p.astype(bf16) for p in jnp.split(out_part, 8, axis=1)])
    w_out_grad = scatter_weight(out_pieces)
    kv_pieces = chunks_to(kv_part.astype(bf16), relative, 0).reshape(-1, kv_width)
    query_kv = jnp.concatenate([query_part.astype(bf16), kv_pieces], axis=1)
    query_kv = scatter_weight(query_kv.reshape(8, -1, query_width + kv_width))
    w_query_grad = query_kv[:, :query_width]
    w_kv_grad = query_kv[:, query_width:].reshape(w_kv.shape)
    gain_parts = jnp.concatenate(
        [
            first_gain_part.reshape(8, -1),
            chunks_to(second_gain_part, relative, 0).reshape(8, -1),
            chunks_to(latent_gain_part, relative, 0).reshape(8, -1),
        ],
        axis=1,
    ).reshape(8, -1, latent_width)
    last = jnp.concatenate([latent_part.reshape(8, -1, latent_width), gain_parts], axis=1)
    last = gather_heads(scatter_weight(last.astype(bf16)).astype(bf16))
    last = rows_absolute(last).reshape(4, -1, latent_width).astype(f32)
    latent_rows = w_latent.shape[0]
    w_latent_grad = jnp.concatenate([last[i, :latent_rows] for i in range(4)], axis=1)
    gains = jnp.sum(last[:, latent_rows:], axis=0).reshape(-1)
    side = D // 8

    out_groups = []
    for hidden_g in hidden_parts:
        half = hidden_g.shape[0] // 2
        pair = tuple(nn(p, down_all).astype(bf16) for p in (hidden_g[:half], hidden_g[half:]))
        out_groups.append(tuple(after(p, grad_attention) for p in pair))
    ffn_own = scatter_rows(out_groups)
    output = rows_absolute(gather_heads((after_attention + ffn_own).astype(bf16)))
    rows_all = jnp.concatenate([p for g in rows for p in g], axis=0)
    grads_all = jnp.concatenate([p[:, :D] for g in grads for p in g], axis=0)
    gate_back = after(jnp.concatenate(gate_parts, axis=0), query_part, kv_part)
    up_back = after(jnp.concatenate(up_parts, axis=0), query_part, kv_part)
    hidden_all = after(jnp.concatenate(hidden_parts, axis=0), query_part, kv_part)
    gate_grad = nn(rows_all.T, gate_back)
    up_grad = nn(rows_all.T, up_back)
    down_grad = nn(hidden_all.T, grads_all)
    shared_first = EXP_LOC * part

    def own_experts(array):
        return jnp.stack([array[:, e * part : e * part + hidden] for e in range(EXP_LOC)])

    expert_down_grad = jnp.stack([down_grad[e * part : e * part + hidden] for e in range(EXP_LOC)])
    shared_stop = shared_first + shared_hidden
    shared_two_grad = lax.all_to_all(
        jnp.stack([gate_grad[:, shared_first:shared_stop], up_grad[:, shared_first:shared_stop]]).astype(bf16),
        PLANE,
        split_axis=1,
        concat_axis=2,
        tiled=True,
    ).astype(f32)
    shared_down_grad = lax.all_to_all(
        down_grad[shared_first:shared_stop].astype(bf16), PLANE, split_axis=1, concat_axis=0, tiled=True
    ).astype(f32)
    return (
        output,
        input_grad,
        gains[:side],
        gains[2 * side :],
        gains[side : 2 * side],
        w_query_grad,
        w_latent_grad,
        w_kv_grad,
        w_out_grad,
        own_experts(gate_grad),
        own_experts(up_grad),
        expert_down_grad,
        shared_two_grad[0],
        shared_two_grad[1],
        shared_down_grad,
    )


def solution(mesh):
    in_specs = (
        P((FSDP, TENSOR), None),
        P((FSDP, TENSOR), None),
        P(),
        P(),
        P(),
        P((FSDP, TENSOR), HEADS),
        P((FSDP, TENSOR), None),
        P((FSDP, TENSOR), HEADS),
        P(HEADS, (FSDP, TENSOR)),
        P((FSDP, HEADS), None, TENSOR),
        P((FSDP, HEADS), None, TENSOR),
        P((FSDP, HEADS), TENSOR, None),
        P((FSDP, HEADS), TENSOR),
        P((FSDP, HEADS), TENSOR),
        P(TENSOR, (FSDP, HEADS)),
        P((FSDP, TENSOR), None),
        P((FSDP, TENSOR), None),
        P((FSDP, TENSOR), None),
    )
    out_specs = (
        P((FSDP, TENSOR), None),
        P((FSDP, TENSOR), None),
        P((FSDP, TENSOR)),
        P((FSDP, TENSOR)),
        P((FSDP, TENSOR)),
        P((FSDP, TENSOR), HEADS),
        P((FSDP, TENSOR), None),
        P((FSDP, TENSOR), HEADS),
        P(HEADS, (FSDP, TENSOR)),
        P((FSDP, HEADS), None, TENSOR),
        P((FSDP, HEADS), None, TENSOR),
        P((FSDP, HEADS), TENSOR, None),
        P((FSDP, HEADS), TENSOR),
        P((FSDP, HEADS), TENSOR),
        P(TENSOR, (FSDP, HEADS)),
    )
    dense = tuple(mesh.shape[a] for a in (FSDP, HEADS, TENSOR)) == (2, 4, 4)
    program = dense_shards if dense else shards
    return jax.shard_map(program, mesh=mesh, in_specs=in_specs, out_specs=out_specs, check_vma=False)
```

```python
import jax
import jax.numpy as jnp
from jax import lax
from jax.sharding import PartitionSpec as P
from jax.experimental import pallas as pl
from jax.experimental.pallas import tpu as pltpu

FSDP = "fsdp"
HEADS = "heads"
TENSOR = "tensor"
SCORE = "qhd,khd->hqk"
MIX = "hqk,khd->qhd"
BACK = "hqk,qhd->khd"

D = 2048
NOPE = 128
ROPE = 64
VDIM = 128
KVR = 512
TOP = 6
EXP_LOC = 2
LEN = 512
SEQ_DEV = 1


epsilon = 1e-06
theta_base = 10000.0


def rms_parts(vector):
    inverse = lax.rsqrt(jnp.mean(vector * vector, axis=-1, keepdims=True) + epsilon)
    return (vector * inverse, inverse)


def rms_back(grad_norm, normed, inverse, gain_vec):
    scaled = grad_norm * gain_vec
    inner_mean = jnp.mean(scaled * normed, axis=-1, keepdims=True)
    return inverse * (scaled - normed * inner_mean)


def rope_tables(row_count):
    half_width = ROPE // 2
    position = (jnp.arange(row_count) % LEN).astype(jnp.float32)
    exponent = jnp.arange(half_width).astype(jnp.float32) * (2.0 / ROPE)
    frequency = theta_base ** (-exponent)
    angles = position[:, None] * frequency[None, :]
    return (jnp.cos(angles), jnp.sin(angles))


def rotate(vector, cosine, sine_table):
    half_width = vector.shape[-1] // 2
    first_half = vector[..., :half_width]
    second_half = vector[..., half_width:]
    return jnp.concatenate(
        [
            first_half * cosine - second_half * sine_table,
            second_half * cosine + first_half * sine_table,
        ],
        axis=-1,
    )


def unrotate(vector, cosine, sine_table):
    half_width = vector.shape[-1] // 2
    first_half = vector[..., :half_width]
    second_half = vector[..., half_width:]
    return jnp.concatenate(
        [
            first_half * cosine + second_half * sine_table,
            second_half * cosine - first_half * sine_table,
        ],
        axis=-1,
    )


def combine(returned, positions, weighting, block_rows):
    width = returned.shape[-1]
    padded = jnp.concatenate(
        [returned.reshape(-1, width), jnp.zeros((1, width), jnp.float32)], axis=0
    )
    summed = jnp.zeros((block_rows, width), jnp.float32)
    for route_index in range(TOP):
        picked = padded[positions[:, route_index]]
        if weighting is None:
            summed = summed + picked
        else:
            summed = summed + picked * weighting[:, route_index : route_index + 1]
    return summed


def dispatch(outgoing):
    return lax.all_to_all(outgoing, (FSDP, HEADS), split_axis=0, concat_axis=0, tiled=True)


def bring_back(host_term, local_term, positions, weighting):
    block_rows = local_term.shape[0]
    arrived_rows = lax.all_to_all(
        host_term.astype(jnp.bfloat16), (FSDP, HEADS), split_axis=0, concat_axis=0, tiled=True
    ).astype(host_term.dtype)
    merged = combine(arrived_rows, positions, weighting, block_rows) + local_term
    own_rows = lax.psum_scatter(
        merged.astype(jnp.bfloat16), TENSOR, scatter_dimension=0, tiled=True
    ).astype(jnp.float32)
    return (
        own_rows,
        lax.all_gather(own_rows.astype(jnp.bfloat16), HEADS, axis=0, tiled=True).astype(
            own_rows.dtype
        ),
    )


def shards(
    block_input,
    cotangent,
    norm1_gain,
    latent_gain,
    norm2_gain,
    w_query,
    w_latent,
    w_kv,
    w_out,
    expert_gate,
    expert_up,
    expert_down,
    shared_gate,
    shared_up,
    shared_down,
    routed_expert_index,
    slots,
    gate_weights,
):
    row_count = block_input.shape[0]
    head_dim = NOPE + ROPE
    local_heads = w_query.shape[1] // head_dim
    score_scale = head_dim ** (-0.5)
    query_full, latent_full, kv_full, out_full = (
        lax.all_gather(w_query, (FSDP, TENSOR), axis=0, tiled=True),
        lax.all_gather(w_latent, (FSDP, TENSOR), axis=0, tiled=True),
        lax.all_gather(w_kv, (FSDP, TENSOR), axis=0, tiled=True),
        lax.all_gather(w_out, (FSDP, TENSOR), axis=1, tiled=True),
    )
    shared_gate_full, shared_up_full, shared_down_full = (
        lax.all_gather(shared_gate, (FSDP, HEADS), axis=0, tiled=True),
        lax.all_gather(shared_up, (FSDP, HEADS), axis=0, tiled=True),
        lax.all_gather(shared_down, (FSDP, HEADS), axis=1, tiled=True),
    )
    residual = block_input.astype(jnp.float32)
    first_normed, first_inverse = rms_parts(residual)
    first_input = (first_normed * norm1_gain).astype(jnp.bfloat16)
    cosine, sine_table = rope_tables(row_count)
    query_raw = jnp.dot(first_input, query_full, preferred_element_type=jnp.float32).reshape(
        row_count, local_heads, head_dim
    )
    queries = jnp.concatenate(
        [
            query_raw[..., :NOPE],
            rotate(query_raw[..., NOPE:], cosine[:, None, :], sine_table[:, None, :]),
        ],
        axis=-1,
    ).astype(jnp.bfloat16)
    latent_raw = jnp.dot(first_input, latent_full, preferred_element_type=jnp.float32)
    latent_normed, latent_inverse = rms_parts(latent_raw[:, :KVR])
    latent_norm = (latent_normed * latent_gain).astype(jnp.bfloat16)
    key_rope = rotate(latent_raw[:, KVR:], cosine, sine_table).astype(jnp.bfloat16)
    key_value = (
        jnp.dot(latent_norm, kv_full, preferred_element_type=jnp.float32)
        .astype(jnp.bfloat16)
        .reshape(row_count, local_heads, NOPE + VDIM)
    )
    key_all = jnp.concatenate(
        [
            key_value[..., :NOPE],
            jnp.broadcast_to(key_rope[:, None, :], (row_count, local_heads, ROPE)),
        ],
        axis=-1,
    )
    values = key_value[..., NOPE:]
    causal = jnp.arange(LEN)[:, None] >= jnp.arange(LEN)[None, :]

    def score_block(queries_s, keys_s):
        scores = (
            jnp.einsum(SCORE, queries_s, keys_s, preferred_element_type=jnp.float32)
            * score_scale
        )
        return jnp.where(causal[None], scores, -1e30)

    def attend(pieces):
        queries_s, keys_s, values_s = pieces
        scores = score_block(queries_s, keys_s)
        highest_score = jnp.max(scores, axis=-1, keepdims=True)
        log_total = highest_score + jnp.log(
            jnp.sum(jnp.exp(scores - highest_score), axis=-1, keepdims=True)
        )
        probabilities = jnp.exp(scores - log_total).astype(jnp.bfloat16)
        context_s = jnp.einsum(
            MIX, probabilities, values_s, preferred_element_type=jnp.float32
        )
        return (context_s.astype(jnp.bfloat16), log_total)

    seq_queries = queries.reshape(SEQ_DEV, LEN, local_heads, head_dim)
    seq_keys = key_all.reshape(SEQ_DEV, LEN, local_heads, head_dim)
    seq_values = values.reshape(SEQ_DEV, LEN, local_heads, VDIM)
    context, log_totals = lax.map(attend, (seq_queries, seq_keys, seq_values))
    context_flat = context.reshape(row_count, local_heads * VDIM)
    attention_part = jnp.dot(context_flat, out_full, preferred_element_type=jnp.float32)
    after_attention = residual + lax.psum(attention_part.astype(jnp.bfloat16), HEADS).astype(
        jnp.float32
    )
    second_normed, second_inverse = rms_parts(after_attention)
    second_input = (second_normed * norm2_gain).astype(jnp.bfloat16)
    quarter = row_count // lax.axis_size(HEADS)
    row_start = lax.axis_index(HEADS) * quarter

    def own_part(array):
        return lax.dynamic_slice_in_dim(array, row_start, quarter, 0)

    tokens_in, grads_in, ids_in, slots_in, gates_in = (
        lax.all_gather(own_part(second_input), TENSOR, axis=0, tiled=True),
        lax.all_gather(own_part(cotangent), TENSOR, axis=0, tiled=True),
        lax.all_gather(own_part(routed_expert_index), TENSOR, axis=0, tiled=True),
        lax.all_gather(own_part(slots), TENSOR, axis=0, tiled=True),
        lax.all_gather(own_part(gate_weights), TENSOR, axis=0, tiled=True),
    )
    hosts = lax.axis_size(FSDP) * lax.axis_size(HEADS)
    experts = EXP_LOC * hosts
    block_rows = tokens_in.shape[0]
    capacity = block_rows * TOP * 5 // (4 * experts)
    positions = jnp.where(slots_in < capacity, ids_in * capacity + slots_in, experts * capacity)
    flat_positions = positions.reshape(-1)
    row_labels = jnp.repeat(jnp.arange(block_rows, dtype=jnp.int32), TOP)
    owners = (
        jnp.full((experts * capacity + 1,), block_rows, jnp.int32)
        .at[flat_positions]
        .set(row_labels)[: experts * capacity]
    )
    routing_gate_weights = gates_in.astype(jnp.float32)
    slot_gates = (
        jnp.zeros((experts * capacity + 1,), jnp.float32)
        .at[flat_positions]
        .set(routing_gate_weights.reshape(-1))[: experts * capacity]
    )
    buffer_shape = (hosts, EXP_LOC, capacity, D)
    tokens_padded = jnp.concatenate([tokens_in, jnp.zeros((1, D), jnp.bfloat16)], axis=0)
    arrived = dispatch(tokens_padded[owners].reshape(buffer_shape))
    gate_act = jnp.einsum(
        "secd,edf->secf", arrived, expert_gate, preferred_element_type=jnp.float32
    )
    up_act = jnp.einsum("secd,edf->secf", arrived, expert_up, preferred_element_type=jnp.float32)
    gate_sigmoid = jax.nn.sigmoid(gate_act)
    gate_silu = gate_act * gate_sigmoid
    expert_hidden = (gate_silu * up_act).astype(jnp.bfloat16)
    expert_out = jnp.einsum(
        "secf,efd->secd", expert_hidden, expert_down, preferred_element_type=jnp.float32
    )
    shared_act = jnp.dot(tokens_in, shared_gate_full, preferred_element_type=jnp.float32)
    shared_lin = jnp.dot(tokens_in, shared_up_full, preferred_element_type=jnp.float32)
    shared_sigmoid = jax.nn.sigmoid(shared_act)
    shared_silu = shared_act * shared_sigmoid
    shared_hidden = (shared_silu * shared_lin).astype(jnp.bfloat16)
    shared_out = jnp.dot(shared_hidden, shared_down_full, preferred_element_type=jnp.float32)
    _, ffn_full = bring_back(expert_out, shared_out, positions, routing_gate_weights)
    output = (after_attention + ffn_full).astype(jnp.bfloat16)
    grads_padded = jnp.concatenate([grads_in, jnp.zeros((1, D), jnp.bfloat16)], axis=0)
    grad_slots = (
        (grads_padded[owners].astype(jnp.float32) * slot_gates[:, None])
        .astype(jnp.bfloat16)
        .reshape(buffer_shape)
    )
    grad_arrived = dispatch(grad_slots)
    grad_hidden = jnp.einsum(
        "secd,efd->secf", grad_arrived, expert_down, preferred_element_type=jnp.float32
    )
    grad_gate = (
        grad_hidden * up_act * gate_sigmoid * (1.0 + gate_act * (1.0 - gate_sigmoid))
    ).astype(jnp.bfloat16)
    grad_up = (grad_hidden * gate_silu).astype(jnp.bfloat16)
    expert_down_grad = jnp.einsum(
        "secf,secd->efd", expert_hidden, grad_arrived, preferred_element_type=jnp.float32
    )
    expert_gate_grad = jnp.einsum(
        "secd,secf->edf", arrived, grad_gate, preferred_element_type=jnp.float32
    )
    expert_up_grad = jnp.einsum(
        "secd,secf->edf", arrived, grad_up, preferred_element_type=jnp.float32
    )
    host_back = jnp.einsum(
        "secf,edf->secd", grad_gate, expert_gate, preferred_element_type=jnp.float32
    ) + jnp.einsum("secf,edf->secd", grad_up, expert_up, preferred_element_type=jnp.float32)
    grad_shared_hidden = jnp.dot(grads_in, shared_down_full.T, preferred_element_type=jnp.float32)
    shared_gate_back = (
        grad_shared_hidden
        * shared_lin
        * shared_sigmoid
        * (1.0 + shared_act * (1.0 - shared_sigmoid))
    ).astype(jnp.bfloat16)
    shared_up_back = (grad_shared_hidden * shared_silu).astype(jnp.bfloat16)
    shared_down_part = jnp.dot(shared_hidden.T, grads_in, preferred_element_type=jnp.float32)
    shared_gate_part = jnp.dot(tokens_in.T, shared_gate_back, preferred_element_type=jnp.float32)
    shared_up_part = jnp.dot(tokens_in.T, shared_up_back, preferred_element_type=jnp.float32)
    shared_gate_grad, shared_up_grad, shared_down_grad = (
        lax.psum_scatter(
            shared_gate_part.astype(jnp.bfloat16),
            (FSDP, HEADS),
            scatter_dimension=0,
            tiled=True,
        ).astype(jnp.float32),
        lax.psum_scatter(
            shared_up_part.astype(jnp.bfloat16), (FSDP, HEADS), scatter_dimension=0, tiled=True
        ).astype(jnp.float32),
        lax.psum_scatter(
            shared_down_part.astype(jnp.bfloat16),
            (FSDP, HEADS),
            scatter_dimension=1,
            tiled=True,
        ).astype(jnp.float32),
    )
    shared_back = jnp.dot(
        shared_gate_back, shared_gate_full.T, preferred_element_type=jnp.float32
    ) + jnp.dot(shared_up_back, shared_up_full.T, preferred_element_type=jnp.float32)
    _, grad_second = bring_back(host_back, shared_back, positions, None)
    second_gain_part = jnp.sum(grad_second * second_normed, axis=0)
    grad_after = cotangent.astype(jnp.float32) + rms_back(
        grad_second, second_normed, second_inverse, norm2_gain
    )
    grad_attention = grad_after.astype(jnp.bfloat16)
    out_part = jnp.dot(context_flat.T, grad_attention, preferred_element_type=jnp.float32)
    grad_context = (
        jnp.dot(grad_attention, out_full.T, preferred_element_type=jnp.float32)
        .astype(jnp.bfloat16)
        .reshape(SEQ_DEV, LEN, local_heads, VDIM)
    )

    def attend_back(pieces):
        queries_s, keys_s, values_s, log_total, grad_context_s = pieces
        scores = score_block(queries_s, keys_s)
        probabilities = jnp.exp(scores - log_total)
        grad_probs = jnp.einsum(
            SCORE, grad_context_s, values_s, preferred_element_type=jnp.float32
        )
        centred = jnp.sum(probabilities * grad_probs, axis=-1, keepdims=True)
        grad_scores = (probabilities * (grad_probs - centred)).astype(jnp.bfloat16)
        grad_queries_s = (
            jnp.einsum(MIX, grad_scores, keys_s, preferred_element_type=jnp.float32)
            * score_scale
        )
        grad_keys_s = (
            jnp.einsum(BACK, grad_scores, queries_s, preferred_element_type=jnp.float32)
            * score_scale
        )
        grad_values_s = jnp.einsum(
            BACK,
            probabilities.astype(jnp.bfloat16),
            grad_context_s,
            preferred_element_type=jnp.float32,
        )
        return (grad_queries_s, grad_keys_s, grad_values_s)

    grad_queries, grad_keys, grad_values = lax.map(
        attend_back, (seq_queries, seq_keys, seq_values, log_totals, grad_context)
    )
    grad_queries = grad_queries.reshape(row_count, local_heads, head_dim)
    grad_keys = grad_keys.reshape(row_count, local_heads, head_dim)
    grad_values = grad_values.reshape(row_count, local_heads, VDIM)
    grad_query_raw = (
        jnp.concatenate(
            [
                grad_queries[..., :NOPE],
                unrotate(grad_queries[..., NOPE:], cosine[:, None, :], sine_table[:, None, :]),
            ],
            axis=-1,
        )
        .astype(jnp.bfloat16)
        .reshape(row_count, local_heads * head_dim)
    )
    query_part = jnp.dot(first_input.T, grad_query_raw, preferred_element_type=jnp.float32)
    first_from_query = jnp.dot(grad_query_raw, query_full.T, preferred_element_type=jnp.float32)
    grad_key_value = (
        jnp.concatenate([grad_keys[..., :NOPE], grad_values], axis=-1)
        .astype(jnp.bfloat16)
        .reshape(row_count, local_heads * (NOPE + VDIM))
    )
    kv_part = jnp.dot(latent_norm.T, grad_key_value, preferred_element_type=jnp.float32)
    grad_latent_norm = jnp.dot(grad_key_value, kv_full.T, preferred_element_type=jnp.float32)
    latent_gain_part = jnp.sum(grad_latent_norm * latent_normed, axis=0)
    grad_compressed = rms_back(grad_latent_norm, latent_normed, latent_inverse, latent_gain)
    grad_key_rope = unrotate(jnp.sum(grad_keys[..., NOPE:], axis=1), cosine, sine_table)
    latent_term = jnp.concatenate([grad_compressed, grad_key_rope], axis=-1)
    first_summed, latent_summed, latent_gain_summed = (
        lax.psum(first_from_query.astype(jnp.bfloat16), HEADS).astype(jnp.float32),
        lax.psum(latent_term.astype(jnp.bfloat16), HEADS).astype(jnp.float32),
        lax.psum(latent_gain_part.astype(jnp.bfloat16), HEADS).astype(jnp.float32),
    )
    grad_latent = latent_summed.astype(jnp.bfloat16)
    latent_part = jnp.dot(first_input.T, grad_latent, preferred_element_type=jnp.float32)
    grad_first = first_summed + jnp.dot(
        grad_latent, latent_full.T, preferred_element_type=jnp.float32
    )
    first_gain_part = jnp.sum(grad_first * first_normed, axis=0)
    input_grad = grad_after + rms_back(grad_first, first_normed, first_inverse, norm1_gain)
    (
        w_query_grad,
        w_latent_grad,
        w_kv_grad,
        w_out_grad,
        norm1_gain_grad,
        latent_gain_grad,
        norm2_gain_grad,
    ) = (
        lax.psum_scatter(
            query_part.astype(jnp.bfloat16), (FSDP, TENSOR), scatter_dimension=0, tiled=True
        ).astype(jnp.float32),
        lax.psum_scatter(
            latent_part.astype(jnp.bfloat16), (FSDP, TENSOR), scatter_dimension=0, tiled=True
        ).astype(jnp.float32),
        lax.psum_scatter(
            kv_part.astype(jnp.bfloat16), (FSDP, TENSOR), scatter_dimension=0, tiled=True
        ).astype(jnp.float32),
        lax.psum_scatter(
            out_part.astype(jnp.bfloat16), (FSDP, TENSOR), scatter_dimension=1, tiled=True
        ).astype(jnp.float32),
        lax.psum_scatter(
            first_gain_part.astype(jnp.bfloat16),
            (FSDP, TENSOR),
            scatter_dimension=0,
            tiled=True,
        ).astype(jnp.float32),
        lax.psum_scatter(
            latent_gain_summed.astype(jnp.bfloat16),
            (FSDP, TENSOR),
            scatter_dimension=0,
            tiled=True,
        ).astype(jnp.float32),
        lax.psum_scatter(
            second_gain_part.astype(jnp.bfloat16),
            (FSDP, TENSOR),
            scatter_dimension=0,
            tiled=True,
        ).astype(jnp.float32),
    )
    return (
        output,
        input_grad,
        norm1_gain_grad,
        latent_gain_grad,
        norm2_gain_grad,
        w_query_grad,
        w_latent_grad,
        w_kv_grad,
        w_out_grad,
        expert_gate_grad,
        expert_up_grad,
        expert_down_grad,
        shared_gate_grad,
        shared_up_grad,
        shared_down_grad,
    )


PLANE = (FSDP, HEADS)
GROUPS = ((0,), (1, 3), (2,))
LANES = 128
TILE = 512
UNIT = 128
bf16 = jnp.bfloat16
f32 = jnp.float32


def after(array, *others):
    return lax.optimization_barrier((array, *others))[0]


def from_tensor(array, k):
    return lax.ppermute(array, TENSOR, [((i + k) % 4, i) for i in range(4)])


def to_tensor(array, k):
    return lax.ppermute(array, TENSOR, [(i, (i + k) % 4) for i in range(4)])


def swap_fsdp(array):
    return lax.ppermute(array, FSDP, [(0, 1), (1, 0)])


def swap_heads(array, mask):
    return lax.ppermute(array, HEADS, [(i, i ^ mask) for i in range(4)])


def swap_plane(array, first):
    pairs = []
    for f in range(2):
        for h in range(4):
            f_to, h_to = (f ^ 1, h) if h % 2 == first else (f, h ^ 2)
            pairs.append((f * 4 + h, f_to * 4 + h_to))
    return lax.ppermute(array, PLANE, pairs)


def gather_rows(unit):
    along = {0: unit}
    for k in (1, 3, 2):
        along[k] = from_tensor(unit, k)
    groups = []
    for group in GROUPS:
        here = jnp.concatenate([along[k] for k in group], axis=0) if len(group) > 1 else along[group[0]]
        first = swap_plane(here, 0)
        second = swap_plane(here, 1)
        mine = [here, first, second, swap_plane(first, 1)]
        groups.append(mine + [swap_heads(p, 1) for p in mine])
    return groups


def scatter_rows(groups):
    total = None
    for group, (mine, other) in zip(GROUPS, groups):
        other = swap_heads(other, 1)
        half = mine.shape[0] // 2
        sent = (mine[half:].astype(f32) + other[half:].astype(f32)).astype(bf16)
        sent = swap_plane(sent, 1)
        part = half // 2
        near = [a[:part].astype(f32) for a in (mine, other, sent)]
        far = [a[part:half].astype(f32) for a in (mine, other)] + [sent[part:].astype(f32)]
        far = swap_plane((far[0] + far[1] + far[2]).astype(bf16), 0)
        summed = near[0] + near[1] + near[2] + far.astype(f32)
        for k, piece in zip(group, jnp.split(summed, len(group), axis=0)):
            if k:
                piece = to_tensor(piece.astype(bf16), k).astype(f32)
            total = piece if total is None else total + piece
    return total


def gather_weight(shard):
    along = {0: shard}
    for k in (1, 3, 2):
        along[k] = from_tensor(shard, k)
    along = [along[k] for k in range(4)]
    return along, [swap_fsdp(p) for p in along]


def scatter_weight(parts):
    parts = [p.astype(bf16) for p in parts]
    summed = {}
    for k in (1, 3, 2, 0):
        far = swap_fsdp(parts[4 + k])
        summed[k] = parts[k].astype(f32) + far.astype(f32)
    total = summed[0]
    for k in (1, 3, 2):
        total = total + to_tensor(summed[k].astype(bf16), k).astype(f32)
    return total


def pick(array, index, count, axis):
    size = array.shape[axis] // count
    return lax.dynamic_slice_in_dim(array, index * size, size, axis)


def nn(left, right):
    return jnp.dot(left, right, preferred_element_type=f32)


def nt(left, right):
    return lax.dot_general(left, right, (((1,), (1,)), ((), ())), preferred_element_type=f32)


def tn(left, right):
    return lax.dot_general(left, right, (((0,), (0,)), ((), ())), preferred_element_type=f32)


def spans(counts, size):
    steps, place = [[]], 0
    for index, count in enumerate(counts):
        row = 0
        while row < count:
            if place == size:
                steps.append([])
                place = 0
            taken = min(count - row, size - place)
            steps[-1].append((index, row, taken, place))
            row += taken
            place += taken
    return steps


def hidden_kernel(first_ref, *refs):
    pieces = 8
    x_refs, g_refs = refs[:pieces], refs[pieces : 2 * pieces]
    gate_ref, up_ref, shared_ref, down_ref = refs[2 * pieces : 2 * pieces + 4]
    d1_ref, d2_ref, h_ref, bg_ref, bu_ref, bs_ref = refs[2 * pieces + 4 : 2 * pieces + 10]
    x_scr, g_scr, sems = refs[2 * pieces + 10 :]
    step = pl.program_id(0)
    half = pl.num_programs(0) // 2
    plan = spans([r.shape[0] for r in x_refs], TILE)

    def copies(j):
        slot = j % 2
        made = []
        for i, (piece, row, count, place) in enumerate(plan[j]):
            for side, (sources, target) in enumerate(((x_refs, x_scr), (g_refs, g_scr))):
                made.append(
                    pltpu.make_async_copy(
                        sources[piece].at[pl.ds(row, count), :],
                        target.at[slot, pl.ds(place, count), :],
                        sems.at[slot, side, i],
                    )
                )
        return made

    @pl.when(step == 0)
    def _():
        for copy in copies(0):
            copy.start()

    for j in range(len(plan)):

        @pl.when(step == j)
        def _(j=j):
            if j + 1 < len(plan):
                for copy in copies(j + 1):
                    copy.start()
            for copy in copies(j):
                copy.wait()

    slot = step % 2
    rows = x_scr[slot]
    routes = g_scr[slot, :, D:].astype(f32)
    routed = gate_ref.shape[0]
    part = routed // EXP_LOC
    lane = lax.broadcasted_iota(jnp.int32, routes.shape, 1)
    scales = [
        jnp.sum(jnp.where(lane == first_ref[0] + e, routes, 0.0), axis=1, keepdims=True)
        for e in range(EXP_LOC)
    ]
    column = lax.broadcasted_iota(jnp.int32, (1, routed), 1)
    scale = jnp.where(column < part, scales[0], scales[1])
    grad_hidden = nt(g_scr[slot, :, :D], down_ref[...])

    def steps(gate_act, up_act, grad, scale):
        sigmoid = jax.nn.sigmoid(gate_act)
        silu = gate_act * sigmoid
        kept = silu * up_act
        if scale is not None:
            kept, grad = kept * scale, grad * scale
        back_gate = grad * up_act * (sigmoid + silu * (1.0 - sigmoid))
        return kept.astype(bf16), back_gate.astype(bf16), (grad * silu).astype(bf16)

    gate_act = nt(rows, gate_ref[...])
    up_act = nt(rows, up_ref[...])
    kept, back_gate, back_up = steps(gate_act, up_act, grad_hidden[:, :routed], scale)
    shared = nt(rows, shared_ref[...])
    kept_s, back_gate_s, back_up_s = steps(
        shared[:, :LANES], shared[:, LANES:], grad_hidden[:, routed:], None
    )
    h_ref[:, :routed] = kept
    h_ref[:, routed:] = kept_s
    bg_ref[...] = back_gate
    bu_ref[...] = back_up
    bs_ref[:, :LANES] = back_gate_s
    bs_ref[:, LANES:] = back_up_s
    result = nn(back_gate, gate_ref[...]) + nn(back_up, up_ref[...])
    result = (result + nn(bs_ref[...], shared_ref[...])).astype(bf16)

    @pl.when(step < half)
    def _():
        d1_ref[...] = result

    @pl.when(step >= half)
    def _():
        d2_ref[...] = result


def hidden_step(first, rows, grads, gate_all, up_all, shared_all, down_all):
    count = 4 * rows[0].shape[0]
    half = count // TILE
    routed = gate_all.shape[0]
    width = down_all.shape[0]

    def near(i, first):
        return (jnp.minimum(i, half - 1), 0)

    def far(i, first):
        return (jnp.maximum(i - half, 0), 0)

    def whole(i, first):
        return (0, 0)

    def step(i, first):
        return (i, 0)

    once = pl.Buffered(1)
    row_shape = jax.ShapeDtypeStruct((count, D), bf16)
    widths = (width, routed, routed, 2 * LANES)
    weights = (gate_all, up_all, shared_all, down_all)
    return pl.pallas_call(
        hidden_kernel,
        out_shape=(row_shape, row_shape)
        + tuple(jax.ShapeDtypeStruct((2 * count, w), bf16) for w in widths),
        grid_spec=pltpu.PrefetchScalarGridSpec(
            num_scalar_prefetch=1,
            grid=(2 * half,),
            in_specs=[pl.BlockSpec(memory_space=pl.ANY)] * (len(rows) + len(grads))
            + [pl.BlockSpec(w.shape, whole, pipeline_mode=once) for w in weights],
            out_specs=[pl.BlockSpec((TILE, D), near), pl.BlockSpec((TILE, D), far)]
            + [pl.BlockSpec((TILE, w), step) for w in widths],
            scratch_shapes=[
                pltpu.VMEM((2, TILE, D), bf16),
                pltpu.VMEM((2, TILE, D + LANES), bf16),
                pltpu.SemaphoreType.DMA((2, 2, TILE // UNIT)),
            ],
        ),
        compiler_params=pltpu.CompilerParams(vmem_limit_bytes=58 * 1024 * 1024),
        cost_estimate=pl.CostEstimate(
            flops=2 * count * D * (3 * routed + width + 4 * LANES + routed) * 2,
            bytes_accessed=2 * count * (3 * D + 3 * width) * 2 + 3 * D * width * 2,
            transcendentals=2 * count * width,
        ),
    )(first, *rows, *grads, *weights)


def weight_grad(lefts, rights, left_start, left_width, shape, dtype=f32):
    places = shape[0]
    stride = left_width // places
    used = shape[1]
    tile = 512
    left_steps = spans([p.shape[0] for p in lefts], tile)
    right_steps = spans([p.shape[0] for p in rights], tile)
    steps = list(zip(left_steps, right_steps))

    def kernel(*refs):
        left_refs, right_refs = refs[: len(lefts)], refs[len(lefts) : len(lefts) + len(rights)]
        out_ref, sum_ref, left_buf, right_buf, left_sems, right_sems = refs[len(lefts) + len(rights) :]

        def copies(i):
            slot = i % 2
            made = []
            for n, (piece, row, count, place) in enumerate(steps[i][0]):
                made.append(
                    pltpu.make_async_copy(
                        left_refs[piece].at[pl.ds(row, count), pl.ds(left_start, left_width)],
                        left_buf.at[slot, pl.ds(place, count), :],
                        left_sems.at[slot, n],
                    )
                )
            for n, (piece, row, count, place) in enumerate(steps[i][1]):
                made.append(
                    pltpu.make_async_copy(
                        right_refs[piece].at[pl.ds(row, count), pl.ds(0, D)],
                        right_buf.at[slot, pl.ds(place, count), :],
                        right_sems.at[slot, n],
                    )
                )
            return made

        for copy in copies(0):
            copy.start()
        for i in range(len(steps)):
            if i + 1 < len(steps):
                for copy in copies(i + 1):
                    copy.start()
            for copy in copies(i):
                copy.wait()
            product = tn(left_buf[i % 2], right_buf[i % 2])
            if i == 0:
                sum_ref[...] = product
            else:
                sum_ref[...] += product
        for e in range(places):
            out_ref[e] = sum_ref[e * stride : e * stride + used, :].astype(dtype)

    return pl.pallas_call(
        kernel,
        out_shape=jax.ShapeDtypeStruct(shape, dtype),
        in_specs=[pl.BlockSpec(memory_space=pl.ANY)] * (len(lefts) + len(rights)),
        out_specs=pl.BlockSpec(memory_space=pltpu.VMEM),
        scratch_shapes=[
            pltpu.VMEM((left_width, D), f32),
            pltpu.VMEM((2, tile, left_width), bf16),
            pltpu.VMEM((2, tile, D), bf16),
            pltpu.SemaphoreType.DMA((2, tile // UNIT)),
            pltpu.SemaphoreType.DMA((2, tile // UNIT)),
        ],
        compiler_params=pltpu.CompilerParams(vmem_limit_bytes=58 * 1024 * 1024),
        cost_estimate=pl.CostEstimate(
            flops=2 * tile * len(steps) * D * left_width,
            bytes_accessed=2 * tile * len(steps) * (D + left_width) + 4 * D * left_width,
            transcendentals=0,
        ),
    )(*lefts, *rights)


def shared_grad(backs, hiddens, rows, grads, hidden_start, used):
    tile = 512
    sources = (backs, rows, hiddens, grads)
    starts = (0, 0, hidden_start, 0)
    widths = (2 * LANES, D, LANES, D)
    plans = [spans([p.shape[0] for p in arrays], tile) for arrays in sources]
    flat = [a for arrays in sources for a in arrays]
    side = D // 8

    def kernel(*refs):
        groups, place = [], 0
        for arrays in sources:
            groups.append(refs[place : place + len(arrays)])
            place += len(arrays)
        out_ref, sum_ref = refs[place], refs[place + 1]
        bufs, sems = refs[place + 2 : place + 6], refs[place + 6]

        def copies(i):
            slot = i % 2
            made = []
            for n, (group, plan) in enumerate(zip(groups, plans)):
                for m, (piece, row, count, target) in enumerate(plan[i]):
                    made.append(
                        pltpu.make_async_copy(
                            group[piece].at[pl.ds(row, count), pl.ds(starts[n], widths[n])],
                            bufs[n].at[slot, pl.ds(target, count), :],
                            sems.at[slot, n, m],
                        )
                    )
            return made

        for copy in copies(0):
            copy.start()
        for i in range(len(plans[0])):
            if i + 1 < len(plans[0]):
                for copy in copies(i + 1):
                    copy.start()
            for copy in copies(i):
                copy.wait()
            slot = i % 2
            first = tn(bufs[0][slot], bufs[1][slot])
            second = tn(bufs[2][slot], bufs[3][slot])
            if i == 0:
                sum_ref[: 2 * LANES] = first
                sum_ref[2 * LANES :] = second
            else:
                sum_ref[: 2 * LANES] += first
                sum_ref[2 * LANES :] += second
        for d in range(8):
            for n in range(3):
                part = sum_ref[n * LANES : n * LANES + used, d * side : (d + 1) * side]
                out_ref[d, n * used : (n + 1) * used, :] = part.astype(bf16)

    return pl.pallas_call(
        kernel,
        out_shape=jax.ShapeDtypeStruct((8, 3 * used, side), bf16),
        in_specs=[pl.BlockSpec(memory_space=pl.ANY)] * len(flat),
        out_specs=pl.BlockSpec(memory_space=pltpu.VMEM),
        scratch_shapes=[pltpu.VMEM((3 * LANES, D), f32)]
        + [pltpu.VMEM((2, tile, w), bf16) for w in widths]
        + [pltpu.SemaphoreType.DMA((2, 4, tile // UNIT))],
        compiler_params=pltpu.CompilerParams(vmem_limit_bytes=58 * 1024 * 1024),
        cost_estimate=pl.CostEstimate(
            flops=2 * tile * len(plans[0]) * D * 3 * LANES,
            bytes_accessed=2 * tile * len(plans[0]) * (2 * D + 3 * LANES),
            transcendentals=0,
        ),
    )(*flat)


def first_kernel(place_ref, x_ref, *refs):
    pieces, (out_ref, w_ref, kv_ref, sems) = refs[:8], refs[8:]
    rows = w_ref.shape[0] // 8
    kv_rows = kv_ref.shape[0] // 8
    copies = []
    for j, piece in enumerate(pieces):
        copies.append(
            pltpu.make_async_copy(
                piece.at[pl.ds(0, rows), :], w_ref.at[pl.ds(j * rows, rows), :], sems.at[0, j]
            )
        )
        start = pl.multiple_of(place_ref[j] * kv_rows, kv_rows)
        copies.append(
            pltpu.make_async_copy(
                piece.at[pl.ds(rows, kv_rows), :], kv_ref.at[pl.ds(start, kv_rows), :], sems.at[1, j]
            )
        )
    for copy in copies:
        copy.start()
    for copy in copies:
        copy.wait()
    out_ref[...] = nn(x_ref[...], w_ref[...])


def first_step(places, rows, pieces, kv_rows):
    side = pieces[0].shape[0] - kv_rows
    width = pieces[0].shape[1]
    vmem = pl.BlockSpec(memory_space=pltpu.VMEM)
    return pl.pallas_call(
        first_kernel,
        out_shape=(
            jax.ShapeDtypeStruct((rows.shape[0], width), f32),
            jax.ShapeDtypeStruct((8 * side, width), bf16),
            jax.ShapeDtypeStruct((8 * kv_rows, width), bf16),
        ),
        in_specs=[pl.BlockSpec(memory_space=pltpu.SMEM), vmem]
        + [pl.BlockSpec(memory_space=pl.ANY)] * 8,
        out_specs=(vmem, vmem, vmem),
        scratch_shapes=[pltpu.SemaphoreType.DMA((2, 8))],
        compiler_params=pltpu.CompilerParams(vmem_limit_bytes=58 * 1024 * 1024),
    )(places, rows, *pieces)


def out_kernel(x_ref, *refs):
    pieces, (kept_ref, sent_ref, w_ref, sems) = refs[:8], refs[8:]
    rows = w_ref.shape[0] // 8
    copies = [
        pltpu.make_async_copy(piece, w_ref.at[pl.ds(j * rows, rows), :], sems.at[j])
        for j, piece in enumerate(pieces)
    ]
    for copy in copies:
        copy.start()
    for copy in copies:
        copy.wait()
    half = kept_ref.shape[0]
    kept_ref[...] = nt(x_ref[:half], w_ref[...])
    sent_ref[...] = nt(x_ref[half:], w_ref[...]).astype(bf16)


def out_step(rows, pieces):
    half = rows.shape[0] // 2
    vmem = pl.BlockSpec(memory_space=pltpu.VMEM)
    return pl.pallas_call(
        out_kernel,
        out_shape=(
            jax.ShapeDtypeStruct((half, D), f32),
            jax.ShapeDtypeStruct((half, D), bf16),
            jax.ShapeDtypeStruct((D, rows.shape[1]), bf16),
        ),
        in_specs=[vmem] + [pl.BlockSpec(memory_space=pl.ANY)] * 8,
        out_specs=(vmem, vmem, vmem),
        scratch_shapes=[pltpu.SemaphoreType.DMA((8,))],
        compiler_params=pltpu.CompilerParams(vmem_limit_bytes=58 * 1024 * 1024),
    )(rows, *pieces)


def pack_kernel(place_ref, x_ref, query_ref, latent_ref, norm_ref, kv_ref, *refs):
    out_refs, kv_scr = refs[:8], refs[8]
    kv_scr[...] = tn(norm_ref[...], kv_ref[...]).astype(bf16)
    rows = x_ref.shape[1] // 8
    query = query_ref.shape[1]
    kv_rows = norm_ref.shape[1] // 8
    for j, out_ref in enumerate(out_refs):
        part = x_ref[:, j * rows : (j + 1) * rows]
        out_ref[:rows, :query] = tn(part, query_ref[...]).astype(bf16)
        out_ref[:rows, query:] = tn(part, latent_ref[...]).astype(bf16)
        start = pl.multiple_of(place_ref[j] * kv_rows, kv_rows)
        out_ref[rows:, :] = kv_scr[pl.ds(start, kv_rows), :]


def pack_step(places, rows, grad_query, grad_latent, latent_norm, grad_kv):
    vmem = pl.BlockSpec(memory_space=pltpu.VMEM)
    width = grad_kv.shape[1]
    count = (rows.shape[1] + latent_norm.shape[1]) // 8
    grad_latent = jnp.pad(
        grad_latent, ((0, 0), (0, width - grad_query.shape[1] - grad_latent.shape[1]))
    )
    return pl.pallas_call(
        pack_kernel,
        out_shape=(jax.ShapeDtypeStruct((count, width), bf16),) * 8,
        in_specs=[pl.BlockSpec(memory_space=pltpu.SMEM)] + [vmem] * 5,
        out_specs=(vmem,) * 8,
        scratch_shapes=[pltpu.VMEM((latent_norm.shape[1], width), bf16)],
        compiler_params=pltpu.CompilerParams(vmem_limit_bytes=58 * 1024 * 1024),
    )(places, rows, grad_query, grad_latent, latent_norm, grad_kv)


def dense_shards(*arrays):
    return dense_layer(*arrays)


def dense_layer(
    block_input,
    cotangent,
    norm1_gain,
    latent_gain,
    norm2_gain,
    w_query,
    w_latent,
    w_kv,
    w_out,
    expert_gate,
    expert_up,
    expert_down,
    shared_gate,
    shared_up,
    shared_down,
    routed_expert_index,
    slots,
    gate_weights,
):
    f = lax.axis_index(FSDP)
    h = lax.axis_index(HEADS)
    t = lax.axis_index(TENSOR)
    row_count = block_input.shape[0]
    head_dim = NOPE + ROPE
    local_heads = w_query.shape[1] // head_dim
    query_width = local_heads * head_dim
    score_scale = head_dim ** (-0.5)
    hosts = lax.axis_size(FSDP) * lax.axis_size(HEADS)
    experts = EXP_LOC * hosts
    capacity = row_count * TOP * 5 // (4 * experts)

    relative = [(f ^ dx) * 4 + (t + k) % 4 for dx in range(2) for k in range(4)]
    absolute = [(F ^ f) * 4 + (T - t) % 4 for F in range(2) for T in range(4)]
    turns = (0, 2, 1, 3)

    def chunks_to(array, order, axis):
        return jnp.concatenate([pick(array, i, 8, axis) for i in order], axis=axis)

    def quarter(array):
        return pick(array, h, 4, 0)

    def rows_relative(array):
        return jnp.concatenate([pick(array, h ^ j, 4, 0) for j in turns], axis=0)

    def rows_absolute(array):
        places = [h ^ i for i in range(4)]
        return jnp.concatenate([pick(array, (p % 2) * 2 + p // 2, 4, 0) for p in places], axis=0)

    def reduce_heads(kept, sent):
        summed = kept + swap_heads(sent.astype(bf16), 1).astype(f32)
        half = summed.shape[0] // 2
        return summed[:half] + swap_heads(summed[half:].astype(bf16), 2).astype(f32)

    def gather_heads(own):
        near = jnp.concatenate([own, swap_heads(own, 2)], axis=0)
        return jnp.concatenate([near, swap_heads(near, 1)], axis=0)

    query_rows = w_query.shape[0]
    latent_width = w_latent.shape[1] // 4
    latent_stop = query_width + latent_width
    kv_width = w_kv.shape[1]

    def fill(piece, axis, size):
        return jnp.pad(piece, [(0, size - piece.shape[axis] if a == axis else 0) for a in range(2)])

    first_pack = jnp.concatenate([w_query, pick(w_latent, h, 4, 1)], axis=1)
    first_pack = jnp.concatenate([fill(first_pack, 1, kv_width), w_kv], axis=0)
    first_along, first_far = gather_weight(first_pack)
    first_parts = first_along + first_far

    own_ids, own_slots, own_gates = quarter(routed_expert_index), quarter(slots), quarter(gate_weights)
    lanes = jnp.arange(LANES)[None, None, :]
    used_route = (own_ids[:, :, None] == lanes) & (own_slots[:, :, None] < capacity)
    route_weights = jnp.sum(jnp.where(used_route, own_gates[:, :, None].astype(f32), 0.0), axis=1)
    cotangent_own = quarter(cotangent)
    grad_unit = jnp.concatenate([cotangent_own, route_weights.astype(bf16)], axis=1)

    hidden = expert_gate.shape[2]
    part = -(-hidden // LANES) * LANES
    shared_own = lax.all_to_all(
        jnp.stack([shared_gate.T, shared_up.T, shared_down]),
        PLANE,
        split_axis=1,
        concat_axis=2,
        tiled=True,
    )
    shared_hidden = shared_own.shape[1]

    def side_by_side(routed):
        return jnp.pad(routed, ((0, 0), (0, part - hidden), (0, 0))).reshape(-1, D)

    gate_all = side_by_side(jnp.swapaxes(expert_gate, 1, 2))
    up_all = side_by_side(jnp.swapaxes(expert_up, 1, 2))
    shared_own = after(shared_own, first_along[1], first_along[3])
    shared_all = jnp.concatenate([fill(shared_own[i], 0, LANES) for i in range(2)], axis=0)
    down_all = jnp.concatenate([side_by_side(expert_down), fill(shared_own[2], 0, LANES)], axis=0)

    residual = chunks_to(block_input, relative, 1).astype(f32)
    gain1 = chunks_to(norm1_gain, relative, 0)
    first_normed, first_inverse = rms_parts(residual)
    first_input = (first_normed * gain1).astype(bf16)
    cosine, sine_table = rope_tables(row_count)
    first_input = after(first_input, gate_all, up_all, shared_all, down_all)
    places = jnp.stack(relative).astype(jnp.int32)
    first_out, w_first, kv_full = first_step(places, first_input, first_parts, w_kv.shape[0])
    w_queries, w_latents = w_first[:, :query_width], w_first[:, query_width:latent_stop]
    latent_own = first_out[:, query_width:latent_stop].astype(bf16).T
    latent_raw = rows_absolute(gather_heads(latent_own)).T.astype(f32)
    query_raw = first_out[:, :query_width].reshape(row_count, local_heads, head_dim)
    queries = jnp.concatenate(
        [
            query_raw[..., :NOPE],
            rotate(query_raw[..., NOPE:], cosine[:, None, :], sine_table[:, None, :]),
        ],
        axis=-1,
    ).astype(bf16)
    latent_normed, latent_inverse = rms_parts(latent_raw[:, :KVR])
    latent_norm = (latent_normed * latent_gain).astype(bf16)
    key_rope = rotate(latent_raw[:, KVR:], cosine, sine_table).astype(bf16)
    key_value = nn(latent_norm, kv_full).astype(bf16).reshape(row_count, local_heads, NOPE + VDIM)
    keys = jnp.concatenate(
        [
            key_value[..., :NOPE],
            jnp.broadcast_to(key_rope[:, None, :], (row_count, local_heads, ROPE)),
        ],
        axis=-1,
    )
    values = key_value[..., NOPE:]
    out_along, out_far = gather_weight(w_out.T)
    causal = jnp.arange(LEN)[:, None] >= jnp.arange(LEN)[None, :]

    def score_block():
        scores = jnp.einsum(SCORE, queries, keys, preferred_element_type=f32) * score_scale
        return jnp.where(causal[None], scores, -1e30)

    scores = score_block()
    highest_score = jnp.max(scores, axis=-1, keepdims=True)
    log_total = highest_score + jnp.log(
        jnp.sum(jnp.exp(scores - highest_score), axis=-1, keepdims=True)
    )
    probabilities = jnp.exp(scores - log_total).astype(bf16)
    context = jnp.einsum(MIX, probabilities, values, preferred_element_type=f32)
    context = rows_relative(context.astype(bf16).reshape(row_count, local_heads * VDIM))
    kept, sent, out_full = out_step(context, out_along + out_far)
    attention_own = reduce_heads(kept, sent)
    after_attention = quarter(block_input).astype(f32) + chunks_to(attention_own, absolute, 1)
    second_normed, second_inverse = rms_parts(after_attention)
    second_input = (second_normed * norm2_gain).astype(bf16)

    rows = gather_rows(second_input)
    grads = gather_rows(grad_unit)
    first_expert = ((f * lax.axis_size(HEADS) + h) * EXP_LOC).astype(jnp.int32).reshape(1)
    grad_groups, hidden_parts, gate_parts, up_parts, shared_parts = [], [], [], [], []
    for rows_g, grads_g in zip(rows, grads):
        near, far, hidden_g, gate_g, up_g, shared_g = hidden_step(
            first_expert, rows_g, grads_g, gate_all, up_all, shared_all, down_all
        )
        grad_groups.append((near, far))
        hidden_parts.append(hidden_g)
        gate_parts.append(gate_g)
        up_parts.append(up_g)
        shared_parts.append(shared_g)
    grad_second = scatter_rows(grad_groups)

    second_gain_part = jnp.sum(grad_second * second_normed, axis=0)
    grad_after = cotangent_own.astype(f32) + rms_back(
        grad_second, second_normed, second_inverse, norm2_gain
    )
    grad_after = chunks_to(grad_after, relative, 1)
    grad_attention = gather_heads(grad_after.astype(bf16))
    out_part = tn(grad_attention, context)
    grad_context = nn(grad_attention, out_full).astype(bf16)
    grad_context = rows_absolute(grad_context).reshape(row_count, local_heads, VDIM)
    probabilities = jnp.exp(score_block() - log_total)
    grad_probs = jnp.einsum(SCORE, grad_context, values, preferred_element_type=f32)
    centred = jnp.sum(probabilities * grad_probs, axis=-1, keepdims=True)
    grad_scores = (probabilities * (grad_probs - centred)).astype(bf16)
    grad_queries = (
        jnp.einsum(MIX, grad_scores, keys, preferred_element_type=f32) * score_scale
    )
    grad_keys = (
        jnp.einsum(BACK, grad_scores, queries, preferred_element_type=f32) * score_scale
    )
    grad_values = jnp.einsum(
        BACK, probabilities.astype(bf16), grad_context, preferred_element_type=f32
    )
    grad_query_raw = (
        jnp.concatenate(
            [
                grad_queries[..., :NOPE],
                unrotate(grad_queries[..., NOPE:], cosine[:, None, :], sine_table[:, None, :]),
            ],
            axis=-1,
        )
        .astype(bf16)
        .reshape(row_count, query_width)
    )
    first_from_query = nt(rows_relative(grad_query_raw), w_queries)
    grad_key_value = (
        jnp.concatenate([grad_keys[..., :NOPE], grad_values], axis=-1)
        .astype(bf16)
        .reshape(row_count, local_heads * (NOPE + VDIM))
    )
    grad_latent_norm = nt(grad_key_value, kv_full)
    latent_gain_part = jnp.sum(grad_latent_norm * latent_normed, axis=0)
    grad_compressed = rms_back(grad_latent_norm, latent_normed, latent_inverse, latent_gain)
    grad_key_rope = unrotate(jnp.sum(grad_keys[..., NOPE:], axis=1), cosine, sine_table)
    latent_term = jnp.concatenate([grad_compressed, grad_key_rope], axis=-1)
    latent_term = rows_relative(latent_term.T)
    half = latent_term.shape[0] // 2
    grad_latent = reduce_heads(latent_term[:half], latent_term[half:]).astype(bf16)
    grad_latent_rows = jnp.concatenate([pick(grad_latent, h ^ j, 4, 1) for j in turns], axis=1)
    first_from_latent = lax.dot_general(
        grad_latent_rows, w_latents, (((0,), (1,)), ((), ())), preferred_element_type=f32
    )
    first_pieces = pack_step(
        places, first_input, grad_query_raw, grad_latent.T, latent_norm, grad_key_value
    )
    grad_first = reduce_heads(
        first_from_query[: row_count // 2] + first_from_latent[: row_count // 2],
        first_from_query[row_count // 2 :] + first_from_latent[row_count // 2 :],
    )
    first_normed_own = quarter(first_normed)
    first_gain_part = jnp.sum(grad_first * first_normed_own, axis=0)
    input_own = grad_after + rms_back(grad_first, first_normed_own, quarter(first_inverse), gain1)
    input_grad = rows_absolute(gather_heads(chunks_to(input_own.astype(bf16), absolute, 1))).astype(f32)

    w_out_grad = scatter_weight(out_part.reshape(8, -1, out_part.shape[1])).T
    first_grad = scatter_weight(first_pieces)
    w_query_grad = first_grad[:query_rows, :query_width]
    w_kv_grad = first_grad[query_rows:]
    gain_parts = jnp.concatenate(
        [
            first_gain_part.reshape(8, -1),
            chunks_to(second_gain_part, relative, 0).reshape(8, -1),
            chunks_to(latent_gain_part, relative, 0).reshape(8, -1),
        ],
        axis=1,
    ).reshape(8, -1, latent_width)
    gain_parts = scatter_weight(gain_parts)
    last = jnp.concatenate([first_grad[:query_rows, query_width:latent_stop], gain_parts], axis=0)
    last = rows_absolute(gather_heads(last.astype(bf16))).reshape(4, -1, latent_width).astype(f32)
    latent_rows = w_latent.shape[0]
    w_latent_grad = jnp.concatenate([last[i, :latent_rows] for i in range(4)], axis=1)
    gains = jnp.sum(last[:, latent_rows:], axis=0).reshape(-1)
    side = D // 8

    out_groups = []
    for hidden_g in hidden_parts:
        half = hidden_g.shape[0] // 2
        pair = tuple(nn(p, down_all).astype(bf16) for p in (hidden_g[:half], hidden_g[half:]))
        out_groups.append(tuple(after(p, grad_attention) for p in pair))
    ffn_own = scatter_rows(out_groups)
    output = rows_absolute(gather_heads((after_attention + ffn_own).astype(bf16)))
    rows_list = [p for g in rows for p in g]
    grads_list = [p for g in grads for p in g]
    routed = EXP_LOC * part
    shared_grads = shared_grad(shared_parts, hidden_parts, rows_list, grads_list, routed, shared_hidden)
    shared_grads = lax.all_to_all(
        after(shared_grads, grad_query_raw), PLANE, split_axis=0, concat_axis=0, tiled=True
    ).reshape(8, 3, shared_hidden, -1)
    shared_grads = [shared_grads[:, i].astype(f32).reshape(8 * shared_hidden, -1) for i in range(3)]
    expert_grads = []
    for lefts, rights in ((gate_parts, rows_list), (up_parts, rows_list), (hidden_parts, grads_list)):
        expert_grads.append(weight_grad(lefts, rights, 0, routed, (EXP_LOC, hidden, D)))
    return (
        output,
        input_grad,
        gains[:side],
        gains[2 * side :],
        gains[side : 2 * side],
        w_query_grad,
        w_latent_grad,
        w_kv_grad,
        w_out_grad,
        jnp.swapaxes(expert_grads[0], 1, 2),
        jnp.swapaxes(expert_grads[1], 1, 2),
        expert_grads[2],
        shared_grads[0].T,
        shared_grads[1].T,
        shared_grads[2],
    )


def solution(mesh):
    in_specs = (
        P((FSDP, TENSOR), None),
        P((FSDP, TENSOR), None),
        P(),
        P(),
        P(),
        P((FSDP, TENSOR), HEADS),
        P((FSDP, TENSOR), None),
        P((FSDP, TENSOR), HEADS),
        P(HEADS, (FSDP, TENSOR)),
        P((FSDP, HEADS), None, TENSOR),
        P((FSDP, HEADS), None, TENSOR),
        P((FSDP, HEADS), TENSOR, None),
        P((FSDP, HEADS), TENSOR),
        P((FSDP, HEADS), TENSOR),
        P(TENSOR, (FSDP, HEADS)),
        P((FSDP, TENSOR), None),
        P((FSDP, TENSOR), None),
        P((FSDP, TENSOR), None),
    )
    out_specs = (
        P((FSDP, TENSOR), None),
        P((FSDP, TENSOR), None),
        P((FSDP, TENSOR)),
        P((FSDP, TENSOR)),
        P((FSDP, TENSOR)),
        P((FSDP, TENSOR), HEADS),
        P((FSDP, TENSOR), None),
        P((FSDP, TENSOR), HEADS),
        P(HEADS, (FSDP, TENSOR)),
        P((FSDP, HEADS), None, TENSOR),
        P((FSDP, HEADS), None, TENSOR),
        P((FSDP, HEADS), TENSOR, None),
        P((FSDP, HEADS), TENSOR),
        P((FSDP, HEADS), TENSOR),
        P(TENSOR, (FSDP, HEADS)),
    )
    dense = tuple(mesh.shape[a] for a in (FSDP, HEADS, TENSOR)) == (2, 4, 4)
    program = dense_shards if dense else shards
    program = jax.shard_map(
        program, mesh=mesh, in_specs=in_specs, out_specs=out_specs, check_vma=False
    )
    return program
```

```python
import jax
import jax.numpy as jnp
from jax import lax
from jax.sharding import PartitionSpec as P
from jax.experimental import pallas as pl
from jax.experimental.pallas import tpu as pltpu

FSDP = "fsdp"
HEADS = "heads"
TENSOR = "tensor"
SCORE = "qhd,khd->hqk"
MIX = "hqk,khd->qhd"
BACK = "hqk,qhd->khd"

D = 2048
NOPE = 128
ROPE = 64
VDIM = 128
KVR = 512
TOP = 6
EXP_LOC = 2
LEN = 512
SEQ_DEV = 1


epsilon = 1e-06
theta_base = 10000.0


def rms_parts(vector):
    inverse = lax.rsqrt(jnp.mean(vector * vector, axis=-1, keepdims=True) + epsilon)
    return (vector * inverse, inverse)


def rms_back(grad_norm, normed, inverse, gain_vec):
    scaled = grad_norm * gain_vec
    inner_mean = jnp.mean(scaled * normed, axis=-1, keepdims=True)
    return inverse * (scaled - normed * inner_mean)


def rope_tables(row_count):
    half_width = ROPE // 2
    position = (jnp.arange(row_count) % LEN).astype(jnp.float32)
    exponent = jnp.arange(half_width).astype(jnp.float32) * (2.0 / ROPE)
    frequency = theta_base ** (-exponent)
    angles = position[:, None] * frequency[None, :]
    return (jnp.cos(angles), jnp.sin(angles))


def rotate(vector, cosine, sine_table):
    half_width = vector.shape[-1] // 2
    first_half = vector[..., :half_width]
    second_half = vector[..., half_width:]
    return jnp.concatenate(
        [
            first_half * cosine - second_half * sine_table,
            second_half * cosine + first_half * sine_table,
        ],
        axis=-1,
    )


def unrotate(vector, cosine, sine_table):
    half_width = vector.shape[-1] // 2
    first_half = vector[..., :half_width]
    second_half = vector[..., half_width:]
    return jnp.concatenate(
        [
            first_half * cosine + second_half * sine_table,
            second_half * cosine - first_half * sine_table,
        ],
        axis=-1,
    )


def combine(returned, positions, weighting, block_rows):
    width = returned.shape[-1]
    padded = jnp.concatenate(
        [returned.reshape(-1, width), jnp.zeros((1, width), jnp.float32)], axis=0
    )
    summed = jnp.zeros((block_rows, width), jnp.float32)
    for route_index in range(TOP):
        picked = padded[positions[:, route_index]]
        if weighting is None:
            summed = summed + picked
        else:
            summed = summed + picked * weighting[:, route_index : route_index + 1]
    return summed


def dispatch(outgoing):
    return lax.all_to_all(outgoing, (FSDP, HEADS), split_axis=0, concat_axis=0, tiled=True)


def bring_back(host_term, local_term, positions, weighting):
    block_rows = local_term.shape[0]
    arrived_rows = lax.all_to_all(
        host_term.astype(jnp.bfloat16), (FSDP, HEADS), split_axis=0, concat_axis=0, tiled=True
    ).astype(host_term.dtype)
    merged = combine(arrived_rows, positions, weighting, block_rows) + local_term
    own_rows = lax.psum_scatter(
        merged.astype(jnp.bfloat16), TENSOR, scatter_dimension=0, tiled=True
    ).astype(jnp.float32)
    return (
        own_rows,
        lax.all_gather(own_rows.astype(jnp.bfloat16), HEADS, axis=0, tiled=True).astype(
            own_rows.dtype
        ),
    )


def shards(
    block_input,
    cotangent,
    norm1_gain,
    latent_gain,
    norm2_gain,
    w_query,
    w_latent,
    w_kv,
    w_out,
    expert_gate,
    expert_up,
    expert_down,
    shared_gate,
    shared_up,
    shared_down,
    routed_expert_index,
    slots,
    gate_weights,
):
    row_count = block_input.shape[0]
    head_dim = NOPE + ROPE
    local_heads = w_query.shape[1] // head_dim
    score_scale = head_dim ** (-0.5)
    query_full, latent_full, kv_full, out_full = (
        lax.all_gather(w_query, (FSDP, TENSOR), axis=0, tiled=True),
        lax.all_gather(w_latent, (FSDP, TENSOR), axis=0, tiled=True),
        lax.all_gather(w_kv, (FSDP, TENSOR), axis=0, tiled=True),
        lax.all_gather(w_out, (FSDP, TENSOR), axis=1, tiled=True),
    )
    shared_gate_full, shared_up_full, shared_down_full = (
        lax.all_gather(shared_gate, (FSDP, HEADS), axis=0, tiled=True),
        lax.all_gather(shared_up, (FSDP, HEADS), axis=0, tiled=True),
        lax.all_gather(shared_down, (FSDP, HEADS), axis=1, tiled=True),
    )
    residual = block_input.astype(jnp.float32)
    first_normed, first_inverse = rms_parts(residual)
    first_input = (first_normed * norm1_gain).astype(jnp.bfloat16)
    cosine, sine_table = rope_tables(row_count)
    query_raw = jnp.dot(first_input, query_full, preferred_element_type=jnp.float32).reshape(
        row_count, local_heads, head_dim
    )
    queries = jnp.concatenate(
        [
            query_raw[..., :NOPE],
            rotate(query_raw[..., NOPE:], cosine[:, None, :], sine_table[:, None, :]),
        ],
        axis=-1,
    ).astype(jnp.bfloat16)
    latent_raw = jnp.dot(first_input, latent_full, preferred_element_type=jnp.float32)
    latent_normed, latent_inverse = rms_parts(latent_raw[:, :KVR])
    latent_norm = (latent_normed * latent_gain).astype(jnp.bfloat16)
    key_rope = rotate(latent_raw[:, KVR:], cosine, sine_table).astype(jnp.bfloat16)
    key_value = (
        jnp.dot(latent_norm, kv_full, preferred_element_type=jnp.float32)
        .astype(jnp.bfloat16)
        .reshape(row_count, local_heads, NOPE + VDIM)
    )
    key_all = jnp.concatenate(
        [
            key_value[..., :NOPE],
            jnp.broadcast_to(key_rope[:, None, :], (row_count, local_heads, ROPE)),
        ],
        axis=-1,
    )
    values = key_value[..., NOPE:]
    causal = jnp.arange(LEN)[:, None] >= jnp.arange(LEN)[None, :]

    def score_block(queries_s, keys_s):
        scores = (
            jnp.einsum(SCORE, queries_s, keys_s, preferred_element_type=jnp.float32)
            * score_scale
        )
        return jnp.where(causal[None], scores, -1e30)

    def attend(pieces):
        queries_s, keys_s, values_s = pieces
        scores = score_block(queries_s, keys_s)
        highest_score = jnp.max(scores, axis=-1, keepdims=True)
        log_total = highest_score + jnp.log(
            jnp.sum(jnp.exp(scores - highest_score), axis=-1, keepdims=True)
        )
        probabilities = jnp.exp(scores - log_total).astype(jnp.bfloat16)
        context_s = jnp.einsum(
            MIX, probabilities, values_s, preferred_element_type=jnp.float32
        )
        return (context_s.astype(jnp.bfloat16), log_total)

    seq_queries = queries.reshape(SEQ_DEV, LEN, local_heads, head_dim)
    seq_keys = key_all.reshape(SEQ_DEV, LEN, local_heads, head_dim)
    seq_values = values.reshape(SEQ_DEV, LEN, local_heads, VDIM)
    context, log_totals = lax.map(attend, (seq_queries, seq_keys, seq_values))
    context_flat = context.reshape(row_count, local_heads * VDIM)
    attention_part = jnp.dot(context_flat, out_full, preferred_element_type=jnp.float32)
    after_attention = residual + lax.psum(attention_part.astype(jnp.bfloat16), HEADS).astype(
        jnp.float32
    )
    second_normed, second_inverse = rms_parts(after_attention)
    second_input = (second_normed * norm2_gain).astype(jnp.bfloat16)
    quarter = row_count // lax.axis_size(HEADS)
    row_start = lax.axis_index(HEADS) * quarter

    def own_part(array):
        return lax.dynamic_slice_in_dim(array, row_start, quarter, 0)

    tokens_in, grads_in, ids_in, slots_in, gates_in = (
        lax.all_gather(own_part(second_input), TENSOR, axis=0, tiled=True),
        lax.all_gather(own_part(cotangent), TENSOR, axis=0, tiled=True),
        lax.all_gather(own_part(routed_expert_index), TENSOR, axis=0, tiled=True),
        lax.all_gather(own_part(slots), TENSOR, axis=0, tiled=True),
        lax.all_gather(own_part(gate_weights), TENSOR, axis=0, tiled=True),
    )
    hosts = lax.axis_size(FSDP) * lax.axis_size(HEADS)
    experts = EXP_LOC * hosts
    block_rows = tokens_in.shape[0]
    capacity = block_rows * TOP * 5 // (4 * experts)
    positions = jnp.where(slots_in < capacity, ids_in * capacity + slots_in, experts * capacity)
    flat_positions = positions.reshape(-1)
    row_labels = jnp.repeat(jnp.arange(block_rows, dtype=jnp.int32), TOP)
    owners = (
        jnp.full((experts * capacity + 1,), block_rows, jnp.int32)
        .at[flat_positions]
        .set(row_labels)[: experts * capacity]
    )
    routing_gate_weights = gates_in.astype(jnp.float32)
    slot_gates = (
        jnp.zeros((experts * capacity + 1,), jnp.float32)
        .at[flat_positions]
        .set(routing_gate_weights.reshape(-1))[: experts * capacity]
    )
    buffer_shape = (hosts, EXP_LOC, capacity, D)
    tokens_padded = jnp.concatenate([tokens_in, jnp.zeros((1, D), jnp.bfloat16)], axis=0)
    arrived = dispatch(tokens_padded[owners].reshape(buffer_shape))
    gate_act = jnp.einsum(
        "secd,edf->secf", arrived, expert_gate, preferred_element_type=jnp.float32
    )
    up_act = jnp.einsum("secd,edf->secf", arrived, expert_up, preferred_element_type=jnp.float32)
    gate_sigmoid = jax.nn.sigmoid(gate_act)
    gate_silu = gate_act * gate_sigmoid
    expert_hidden = (gate_silu * up_act).astype(jnp.bfloat16)
    expert_out = jnp.einsum(
        "secf,efd->secd", expert_hidden, expert_down, preferred_element_type=jnp.float32
    )
    shared_act = jnp.dot(tokens_in, shared_gate_full, preferred_element_type=jnp.float32)
    shared_lin = jnp.dot(tokens_in, shared_up_full, preferred_element_type=jnp.float32)
    shared_sigmoid = jax.nn.sigmoid(shared_act)
    shared_silu = shared_act * shared_sigmoid
    shared_hidden = (shared_silu * shared_lin).astype(jnp.bfloat16)
    shared_out = jnp.dot(shared_hidden, shared_down_full, preferred_element_type=jnp.float32)
    _, ffn_full = bring_back(expert_out, shared_out, positions, routing_gate_weights)
    output = (after_attention + ffn_full).astype(jnp.bfloat16)
    grads_padded = jnp.concatenate([grads_in, jnp.zeros((1, D), jnp.bfloat16)], axis=0)
    grad_slots = (
        (grads_padded[owners].astype(jnp.float32) * slot_gates[:, None])
        .astype(jnp.bfloat16)
        .reshape(buffer_shape)
    )
    grad_arrived = dispatch(grad_slots)
    grad_hidden = jnp.einsum(
        "secd,efd->secf", grad_arrived, expert_down, preferred_element_type=jnp.float32
    )
    grad_gate = (
        grad_hidden * up_act * gate_sigmoid * (1.0 + gate_act * (1.0 - gate_sigmoid))
    ).astype(jnp.bfloat16)
    grad_up = (grad_hidden * gate_silu).astype(jnp.bfloat16)
    expert_down_grad = jnp.einsum(
        "secf,secd->efd", expert_hidden, grad_arrived, preferred_element_type=jnp.float32
    )
    expert_gate_grad = jnp.einsum(
        "secd,secf->edf", arrived, grad_gate, preferred_element_type=jnp.float32
    )
    expert_up_grad = jnp.einsum(
        "secd,secf->edf", arrived, grad_up, preferred_element_type=jnp.float32
    )
    host_back = jnp.einsum(
        "secf,edf->secd", grad_gate, expert_gate, preferred_element_type=jnp.float32
    ) + jnp.einsum("secf,edf->secd", grad_up, expert_up, preferred_element_type=jnp.float32)
    grad_shared_hidden = jnp.dot(grads_in, shared_down_full.T, preferred_element_type=jnp.float32)
    shared_gate_back = (
        grad_shared_hidden
        * shared_lin
        * shared_sigmoid
        * (1.0 + shared_act * (1.0 - shared_sigmoid))
    ).astype(jnp.bfloat16)
    shared_up_back = (grad_shared_hidden * shared_silu).astype(jnp.bfloat16)
    shared_down_part = jnp.dot(shared_hidden.T, grads_in, preferred_element_type=jnp.float32)
    shared_gate_part = jnp.dot(tokens_in.T, shared_gate_back, preferred_element_type=jnp.float32)
    shared_up_part = jnp.dot(tokens_in.T, shared_up_back, preferred_element_type=jnp.float32)
    shared_gate_grad, shared_up_grad, shared_down_grad = (
        lax.psum_scatter(
            shared_gate_part.astype(jnp.bfloat16),
            (FSDP, HEADS),
            scatter_dimension=0,
            tiled=True,
        ).astype(jnp.float32),
        lax.psum_scatter(
            shared_up_part.astype(jnp.bfloat16), (FSDP, HEADS), scatter_dimension=0, tiled=True
        ).astype(jnp.float32),
        lax.psum_scatter(
            shared_down_part.astype(jnp.bfloat16),
            (FSDP, HEADS),
            scatter_dimension=1,
            tiled=True,
        ).astype(jnp.float32),
    )
    shared_back = jnp.dot(
        shared_gate_back, shared_gate_full.T, preferred_element_type=jnp.float32
    ) + jnp.dot(shared_up_back, shared_up_full.T, preferred_element_type=jnp.float32)
    _, grad_second = bring_back(host_back, shared_back, positions, None)
    second_gain_part = jnp.sum(grad_second * second_normed, axis=0)
    grad_after = cotangent.astype(jnp.float32) + rms_back(
        grad_second, second_normed, second_inverse, norm2_gain
    )
    grad_attention = grad_after.astype(jnp.bfloat16)
    out_part = jnp.dot(context_flat.T, grad_attention, preferred_element_type=jnp.float32)
    grad_context = (
        jnp.dot(grad_attention, out_full.T, preferred_element_type=jnp.float32)
        .astype(jnp.bfloat16)
        .reshape(SEQ_DEV, LEN, local_heads, VDIM)
    )

    def attend_back(pieces):
        queries_s, keys_s, values_s, log_total, grad_context_s = pieces
        scores = score_block(queries_s, keys_s)
        probabilities = jnp.exp(scores - log_total)
        grad_probs = jnp.einsum(
            SCORE, grad_context_s, values_s, preferred_element_type=jnp.float32
        )
        centred = jnp.sum(probabilities * grad_probs, axis=-1, keepdims=True)
        grad_scores = (probabilities * (grad_probs - centred)).astype(jnp.bfloat16)
        grad_queries_s = (
            jnp.einsum(MIX, grad_scores, keys_s, preferred_element_type=jnp.float32)
            * score_scale
        )
        grad_keys_s = (
            jnp.einsum(BACK, grad_scores, queries_s, preferred_element_type=jnp.float32)
            * score_scale
        )
        grad_values_s = jnp.einsum(
            BACK,
            probabilities.astype(jnp.bfloat16),
            grad_context_s,
            preferred_element_type=jnp.float32,
        )
        return (grad_queries_s, grad_keys_s, grad_values_s)

    grad_queries, grad_keys, grad_values = lax.map(
        attend_back, (seq_queries, seq_keys, seq_values, log_totals, grad_context)
    )
    grad_queries = grad_queries.reshape(row_count, local_heads, head_dim)
    grad_keys = grad_keys.reshape(row_count, local_heads, head_dim)
    grad_values = grad_values.reshape(row_count, local_heads, VDIM)
    grad_query_raw = (
        jnp.concatenate(
            [
                grad_queries[..., :NOPE],
                unrotate(grad_queries[..., NOPE:], cosine[:, None, :], sine_table[:, None, :]),
            ],
            axis=-1,
        )
        .astype(jnp.bfloat16)
        .reshape(row_count, local_heads * head_dim)
    )
    query_part = jnp.dot(first_input.T, grad_query_raw, preferred_element_type=jnp.float32)
    first_from_query = jnp.dot(grad_query_raw, query_full.T, preferred_element_type=jnp.float32)
    grad_key_value = (
        jnp.concatenate([grad_keys[..., :NOPE], grad_values], axis=-1)
        .astype(jnp.bfloat16)
        .reshape(row_count, local_heads * (NOPE + VDIM))
    )
    kv_part = jnp.dot(latent_norm.T, grad_key_value, preferred_element_type=jnp.float32)
    grad_latent_norm = jnp.dot(grad_key_value, kv_full.T, preferred_element_type=jnp.float32)
    latent_gain_part = jnp.sum(grad_latent_norm * latent_normed, axis=0)
    grad_compressed = rms_back(grad_latent_norm, latent_normed, latent_inverse, latent_gain)
    grad_key_rope = unrotate(jnp.sum(grad_keys[..., NOPE:], axis=1), cosine, sine_table)
    latent_term = jnp.concatenate([grad_compressed, grad_key_rope], axis=-1)
    first_summed, latent_summed, latent_gain_summed = (
        lax.psum(first_from_query.astype(jnp.bfloat16), HEADS).astype(jnp.float32),
        lax.psum(latent_term.astype(jnp.bfloat16), HEADS).astype(jnp.float32),
        lax.psum(latent_gain_part.astype(jnp.bfloat16), HEADS).astype(jnp.float32),
    )
    grad_latent = latent_summed.astype(jnp.bfloat16)
    latent_part = jnp.dot(first_input.T, grad_latent, preferred_element_type=jnp.float32)
    grad_first = first_summed + jnp.dot(
        grad_latent, latent_full.T, preferred_element_type=jnp.float32
    )
    first_gain_part = jnp.sum(grad_first * first_normed, axis=0)
    input_grad = grad_after + rms_back(grad_first, first_normed, first_inverse, norm1_gain)
    (
        w_query_grad,
        w_latent_grad,
        w_kv_grad,
        w_out_grad,
        norm1_gain_grad,
        latent_gain_grad,
        norm2_gain_grad,
    ) = (
        lax.psum_scatter(
            query_part.astype(jnp.bfloat16), (FSDP, TENSOR), scatter_dimension=0, tiled=True
        ).astype(jnp.float32),
        lax.psum_scatter(
            latent_part.astype(jnp.bfloat16), (FSDP, TENSOR), scatter_dimension=0, tiled=True
        ).astype(jnp.float32),
        lax.psum_scatter(
            kv_part.astype(jnp.bfloat16), (FSDP, TENSOR), scatter_dimension=0, tiled=True
        ).astype(jnp.float32),
        lax.psum_scatter(
            out_part.astype(jnp.bfloat16), (FSDP, TENSOR), scatter_dimension=1, tiled=True
        ).astype(jnp.float32),
        lax.psum_scatter(
            first_gain_part.astype(jnp.bfloat16),
            (FSDP, TENSOR),
            scatter_dimension=0,
            tiled=True,
        ).astype(jnp.float32),
        lax.psum_scatter(
            latent_gain_summed.astype(jnp.bfloat16),
            (FSDP, TENSOR),
            scatter_dimension=0,
            tiled=True,
        ).astype(jnp.float32),
        lax.psum_scatter(
            second_gain_part.astype(jnp.bfloat16),
            (FSDP, TENSOR),
            scatter_dimension=0,
            tiled=True,
        ).astype(jnp.float32),
    )
    return (
        output,
        input_grad,
        norm1_gain_grad,
        latent_gain_grad,
        norm2_gain_grad,
        w_query_grad,
        w_latent_grad,
        w_kv_grad,
        w_out_grad,
        expert_gate_grad,
        expert_up_grad,
        expert_down_grad,
        shared_gate_grad,
        shared_up_grad,
        shared_down_grad,
    )


PLANE = (FSDP, HEADS)
GROUPS = (0, 1, 2, 3)
LANES = 128
TILE = 512
UNIT = 128
bf16 = jnp.bfloat16
f32 = jnp.float32


def after(array, *others):
    return lax.optimization_barrier((array, *others))[0]


def from_tensor(array, k):
    return lax.ppermute(array, TENSOR, [((i + k) % 4, i) for i in range(4)])


def to_tensor(array, k):
    return lax.ppermute(array, TENSOR, [(i, (i + k) % 4) for i in range(4)])


def swap_fsdp(array):
    return lax.ppermute(array, FSDP, [(0, 1), (1, 0)])


def swap_heads(array, mask):
    return lax.ppermute(array, HEADS, [(i, i ^ mask) for i in range(4)])


def swap_plane(array, first):
    pairs = []
    for f in range(2):
        for h in range(4):
            f_to, h_to = (f ^ 1, h) if h % 2 == first else (f, h ^ 2)
            pairs.append((f * 4 + h, f_to * 4 + h_to))
    return lax.ppermute(array, PLANE, pairs)


def gather_rows(unit):
    along = {0: unit}
    for k in GROUPS[1:]:
        along[k] = from_tensor(unit, k)
    groups = []
    for group in GROUPS:
        here = along[group]
        first = swap_plane(here, 0)
        second = swap_plane(here, 1)
        mine = [here, first, second, swap_plane(first, 1)]
        groups.append(mine + [swap_heads(p, 1) for p in mine])
    return groups


def scatter_rows(groups, holds=()):
    total = None
    for g, (group, (mine, other)) in enumerate(zip(GROUPS, groups)):
        other = swap_heads(other, 1)
        half = mine.shape[0] // 2
        sent = (mine[half:].astype(f32) + other[half:].astype(f32)).astype(bf16)
        sent = swap_plane(sent, 1)
        part = half // 2
        near = [a[:part].astype(f32) for a in (mine, other, sent)]
        far = [a[part:half].astype(f32) for a in (mine, other)] + [sent[part:].astype(f32)]
        far = swap_plane((far[0] + far[1] + far[2]).astype(bf16), 0)
        if g < len(holds):
            far = after(far, holds[g])
        summed = near[0] + near[1] + near[2] + far.astype(f32)
        if group:
            summed = to_tensor(summed.astype(bf16), group).astype(f32)
        total = summed if total is None else total + summed
    return total


def gather_weight(shard):
    along = {0: shard}
    for k in (1, 3, 2):
        along[k] = from_tensor(shard, k)
    along = [along[k] for k in range(4)]
    return along, [swap_fsdp(p) for p in along]


def scatter_weight(parts, hold=None, end=None):
    parts = [p.astype(bf16) for p in parts]
    summed = {}
    for k in (1, 3, 2, 0):
        far = swap_fsdp(parts[4 + k])
        far = far if hold is None else after(far, hold)
        summed[k] = parts[k].astype(f32) + far.astype(f32)
    total = summed[0]
    for k in (1, 3, 2):
        far = to_tensor(summed[k].astype(bf16), k)
        total = total + (far if end is None else after(far, end)).astype(f32)
    return total


def pick(array, index, count, axis):
    size = array.shape[axis] // count
    return lax.dynamic_slice_in_dim(array, index * size, size, axis)


def nn(left, right):
    return jnp.dot(left, right, preferred_element_type=f32)


def nt(left, right):
    return lax.dot_general(left, right, (((1,), (1,)), ((), ())), preferred_element_type=f32)


def tn(left, right):
    return lax.dot_general(left, right, (((0,), (0,)), ((), ())), preferred_element_type=f32)


def spans(counts, size):
    steps, place = [[]], 0
    for index, count in enumerate(counts):
        row = 0
        while row < count:
            if place == size:
                steps.append([])
                place = 0
            taken = min(count - row, size - place)
            steps[-1].append((index, row, taken, place))
            row += taken
            place += taken
    return steps


def hidden_kernel(first_ref, *refs):
    pieces = 8
    x_refs, g_refs = refs[:pieces], refs[pieces : 2 * pieces]
    gate_ref, up_ref, shared_ref, down_ref = refs[2 * pieces : 2 * pieces + 4]
    d1_ref, d2_ref, y1_ref, y2_ref, h_ref, bg_ref, bu_ref, bs_ref = refs[
        2 * pieces + 4 : 2 * pieces + 12
    ]
    x_scr, g_scr, sems = refs[2 * pieces + 12 :]
    step = pl.program_id(0)
    half = pl.num_programs(0) // 2
    plan = spans([r.shape[0] for r in x_refs], TILE)

    def copies(j):
        slot = j % 2
        made = []
        for i, (piece, row, count, place) in enumerate(plan[j]):
            for side, (sources, target) in enumerate(((x_refs, x_scr), (g_refs, g_scr))):
                made.append(
                    pltpu.make_async_copy(
                        sources[piece].at[pl.ds(row, count), :],
                        target.at[slot, pl.ds(place, count), :],
                        sems.at[slot, side, i],
                    )
                )
        return made

    @pl.when(step == 0)
    def _():
        for copy in copies(0):
            copy.start()

    for j in range(len(plan)):

        @pl.when(step == j)
        def _(j=j):
            if j + 1 < len(plan):
                for copy in copies(j + 1):
                    copy.start()
            for copy in copies(j):
                copy.wait()

    slot = step % 2
    rows = x_scr[slot]
    routes = g_scr[slot, :, D:].astype(f32)
    routed = gate_ref.shape[0]
    part = routed // EXP_LOC
    lane = lax.broadcasted_iota(jnp.int32, routes.shape, 1)
    scales = [
        jnp.sum(jnp.where(lane == first_ref[0] + e, routes, 0.0), axis=1, keepdims=True)
        for e in range(EXP_LOC)
    ]
    column = lax.broadcasted_iota(jnp.int32, (1, routed), 1)
    scale = jnp.where(column < part, scales[0], scales[1])
    grad_hidden = nt(g_scr[slot, :, :D], down_ref[...])

    def steps(gate_act, up_act, grad, scale):
        sigmoid = jax.nn.sigmoid(gate_act)
        silu = gate_act * sigmoid
        kept = silu * up_act
        if scale is not None:
            kept, grad = kept * scale, grad * scale
        back_gate = grad * up_act * (sigmoid + silu * (1.0 - sigmoid))
        return kept.astype(bf16), back_gate.astype(bf16), (grad * silu).astype(bf16)

    gate_act = nt(rows, gate_ref[...])
    up_act = nt(rows, up_ref[...])
    kept, back_gate, back_up = steps(gate_act, up_act, grad_hidden[:, :routed], scale)
    shared = nt(rows, shared_ref[...])
    kept_s, back_gate_s, back_up_s = steps(
        shared[:, :LANES], shared[:, LANES:], grad_hidden[:, routed:], None
    )
    h_ref[:, :routed] = kept
    h_ref[:, routed:] = kept_s
    bg_ref[...] = back_gate
    bu_ref[...] = back_up
    bs_ref[:, :LANES] = back_gate_s
    bs_ref[:, LANES:] = back_up_s
    result = nn(back_gate, gate_ref[...]) + nn(back_up, up_ref[...])
    result = (result + nn(bs_ref[...], shared_ref[...])).astype(bf16)

    out = nn(h_ref[...], down_ref[...]).astype(bf16)

    @pl.when(step < half)
    def _():
        d1_ref[...] = result
        y1_ref[...] = out

    @pl.when(step >= half)
    def _():
        d2_ref[...] = result
        y2_ref[...] = out


def hidden_step(first, rows, grads, gate_all, up_all, shared_all, down_all):
    count = 4 * rows[0].shape[0]
    half = count // TILE
    routed = gate_all.shape[0]
    width = down_all.shape[0]

    def near(i, first):
        return (jnp.minimum(i, half - 1), 0)

    def far(i, first):
        return (jnp.maximum(i - half, 0), 0)

    def whole(i, first):
        return (0, 0)

    def step(i, first):
        return (i, 0)

    once = pl.Buffered(1)
    row_shape = jax.ShapeDtypeStruct((count, D), bf16)
    widths = (width, routed, routed, 2 * LANES)
    weights = (gate_all, up_all, shared_all, down_all)
    return pl.pallas_call(
        hidden_kernel,
        out_shape=(row_shape,) * 4
        + tuple(jax.ShapeDtypeStruct((2 * count, w), bf16) for w in widths),
        grid_spec=pltpu.PrefetchScalarGridSpec(
            num_scalar_prefetch=1,
            grid=(2 * half,),
            in_specs=[pl.BlockSpec(memory_space=pl.ANY)] * (len(rows) + len(grads))
            + [pl.BlockSpec(w.shape, whole, pipeline_mode=once) for w in weights],
            out_specs=[pl.BlockSpec((TILE, D), near), pl.BlockSpec((TILE, D), far)] * 2
            + [pl.BlockSpec((TILE, w), step) for w in widths],
            scratch_shapes=[
                pltpu.VMEM((2, TILE, D), bf16),
                pltpu.VMEM((2, TILE, D + LANES), bf16),
                pltpu.SemaphoreType.DMA((2, 2, TILE // UNIT)),
            ],
        ),
        compiler_params=pltpu.CompilerParams(vmem_limit_bytes=58 * 1024 * 1024),
        cost_estimate=pl.CostEstimate(
            flops=2 * count * D * (3 * routed + 2 * width + 4 * LANES + routed) * 2,
            bytes_accessed=2 * count * (3 * D + 3 * width) * 2 + 3 * D * width * 2,
            transcendentals=2 * count * width,
        ),
    )(first, *rows, *grads, *weights)


def weight_grad(lefts, rights, left_start, left_width, shape, dtype=f32):
    places = shape[0]
    stride = left_width // places
    used = shape[1]
    tile = 512
    left_steps = spans([p.shape[0] for p in lefts], tile)
    right_steps = spans([p.shape[0] for p in rights], tile)
    steps = list(zip(left_steps, right_steps))

    def kernel(*refs):
        left_refs, right_refs = refs[: len(lefts)], refs[len(lefts) : len(lefts) + len(rights)]
        out_ref, sum_ref, left_buf, right_buf, left_sems, right_sems = refs[len(lefts) + len(rights) :]

        def copies(i):
            slot = i % 2
            made = []
            for n, (piece, row, count, place) in enumerate(steps[i][0]):
                made.append(
                    pltpu.make_async_copy(
                        left_refs[piece].at[pl.ds(row, count), pl.ds(left_start, left_width)],
                        left_buf.at[slot, pl.ds(place, count), :],
                        left_sems.at[slot, n],
                    )
                )
            for n, (piece, row, count, place) in enumerate(steps[i][1]):
                made.append(
                    pltpu.make_async_copy(
                        right_refs[piece].at[pl.ds(row, count), pl.ds(0, D)],
                        right_buf.at[slot, pl.ds(place, count), :],
                        right_sems.at[slot, n],
                    )
                )
            return made

        for copy in copies(0):
            copy.start()
        for i in range(len(steps)):
            if i + 1 < len(steps):
                for copy in copies(i + 1):
                    copy.start()
            for copy in copies(i):
                copy.wait()
            product = tn(left_buf[i % 2], right_buf[i % 2])
            if i == 0:
                sum_ref[...] = product
            else:
                sum_ref[...] += product
        for e in range(places):
            out_ref[e] = sum_ref[e * stride : e * stride + used, :].astype(dtype)

    return pl.pallas_call(
        kernel,
        out_shape=jax.ShapeDtypeStruct(shape, dtype),
        in_specs=[pl.BlockSpec(memory_space=pl.ANY)] * (len(lefts) + len(rights)),
        out_specs=pl.BlockSpec(memory_space=pltpu.VMEM),
        scratch_shapes=[
            pltpu.VMEM((left_width, D), f32),
            pltpu.VMEM((2, tile, left_width), bf16),
            pltpu.VMEM((2, tile, D), bf16),
            pltpu.SemaphoreType.DMA((2, tile // UNIT)),
            pltpu.SemaphoreType.DMA((2, tile // UNIT)),
        ],
        compiler_params=pltpu.CompilerParams(vmem_limit_bytes=58 * 1024 * 1024),
        cost_estimate=pl.CostEstimate(
            flops=2 * tile * len(steps) * D * left_width,
            bytes_accessed=2 * tile * len(steps) * (D + left_width) + 4 * D * left_width,
            transcendentals=0,
        ),
    )(*lefts, *rights)


def shared_grad(backs, hiddens, rows, grads, hidden_start, used):
    tile = 512
    sources = (backs, rows, hiddens, grads)
    starts = (0, 0, hidden_start, 0)
    widths = (2 * LANES, D, LANES, D)
    plans = [spans([p.shape[0] for p in arrays], tile) for arrays in sources]
    flat = [a for arrays in sources for a in arrays]
    side = D // 8

    def kernel(*refs):
        groups, place = [], 0
        for arrays in sources:
            groups.append(refs[place : place + len(arrays)])
            place += len(arrays)
        out_ref, sum_ref = refs[place], refs[place + 1]
        bufs, sems = refs[place + 2 : place + 6], refs[place + 6]

        def copies(i):
            slot = i % 2
            made = []
            for n, (group, plan) in enumerate(zip(groups, plans)):
                for m, (piece, row, count, target) in enumerate(plan[i]):
                    made.append(
                        pltpu.make_async_copy(
                            group[piece].at[pl.ds(row, count), pl.ds(starts[n], widths[n])],
                            bufs[n].at[slot, pl.ds(target, count), :],
                            sems.at[slot, n, m],
                        )
                    )
            return made

        for copy in copies(0):
            copy.start()
        for i in range(len(plans[0])):
            if i + 1 < len(plans[0]):
                for copy in copies(i + 1):
                    copy.start()
            for copy in copies(i):
                copy.wait()
            slot = i % 2
            first = tn(bufs[0][slot], bufs[1][slot])
            second = tn(bufs[2][slot], bufs[3][slot])
            if i == 0:
                sum_ref[: 2 * LANES] = first
                sum_ref[2 * LANES :] = second
            else:
                sum_ref[: 2 * LANES] += first
                sum_ref[2 * LANES :] += second
        for d in range(8):
            for n in range(3):
                part = sum_ref[n * LANES : n * LANES + used, d * side : (d + 1) * side]
                out_ref[d, n * used : (n + 1) * used, :] = part.astype(bf16)

    return pl.pallas_call(
        kernel,
        out_shape=jax.ShapeDtypeStruct((8, 3 * used, side), bf16),
        in_specs=[pl.BlockSpec(memory_space=pl.ANY)] * len(flat),
        out_specs=pl.BlockSpec(memory_space=pltpu.VMEM),
        scratch_shapes=[pltpu.VMEM((3 * LANES, D), f32)]
        + [pltpu.VMEM((2, tile, w), bf16) for w in widths]
        + [pltpu.SemaphoreType.DMA((2, 4, tile // UNIT))],
        compiler_params=pltpu.CompilerParams(vmem_limit_bytes=58 * 1024 * 1024),
        cost_estimate=pl.CostEstimate(
            flops=2 * tile * len(plans[0]) * D * 3 * LANES,
            bytes_accessed=2 * tile * len(plans[0]) * (2 * D + 3 * LANES),
            transcendentals=0,
        ),
    )(*flat)


def first_kernel(place_ref, x_ref, *refs):
    pieces, (out_ref, w_ref, kv_ref, sems) = refs[:8], refs[8:]
    rows = w_ref.shape[0] // 8
    kv_rows = kv_ref.shape[0] // 8
    copies = []
    for j, piece in enumerate(pieces):
        copies.append(
            pltpu.make_async_copy(
                piece.at[pl.ds(0, rows), :], w_ref.at[pl.ds(j * rows, rows), :], sems.at[0, j]
            )
        )
        start = pl.multiple_of(place_ref[j] * kv_rows, kv_rows)
        copies.append(
            pltpu.make_async_copy(
                piece.at[pl.ds(rows, kv_rows), :], kv_ref.at[pl.ds(start, kv_rows), :], sems.at[1, j]
            )
        )
    for copy in copies:
        copy.start()
    for copy in copies:
        copy.wait()
    out_ref[...] = nn(x_ref[...], w_ref[...])


def first_step(places, rows, pieces, kv_rows):
    side = pieces[0].shape[0] - kv_rows
    width = pieces[0].shape[1]
    vmem = pl.BlockSpec(memory_space=pltpu.VMEM)
    return pl.pallas_call(
        first_kernel,
        out_shape=(
            jax.ShapeDtypeStruct((rows.shape[0], width), f32),
            jax.ShapeDtypeStruct((8 * side, width), bf16),
            jax.ShapeDtypeStruct((8 * kv_rows, width), bf16),
        ),
        in_specs=[pl.BlockSpec(memory_space=pltpu.SMEM), vmem]
        + [pl.BlockSpec(memory_space=pl.ANY)] * 8,
        out_specs=(vmem, vmem, vmem),
        scratch_shapes=[pltpu.SemaphoreType.DMA((2, 8))],
        compiler_params=pltpu.CompilerParams(vmem_limit_bytes=58 * 1024 * 1024),
    )(places, rows, *pieces)


def out_kernel(x_ref, *refs):
    pieces, (kept_ref, sent_ref, w_ref, sems) = refs[:8], refs[8:]
    rows = w_ref.shape[0] // 8
    copies = [
        pltpu.make_async_copy(piece, w_ref.at[pl.ds(j * rows, rows), :], sems.at[j])
        for j, piece in enumerate(pieces)
    ]
    for copy in copies:
        copy.start()
    for copy in copies:
        copy.wait()
    half = kept_ref.shape[0]
    kept_ref[...] = nt(x_ref[:half], w_ref[...])
    sent_ref[...] = nt(x_ref[half:], w_ref[...]).astype(bf16)


def out_step(rows, pieces):
    half = rows.shape[0] // 2
    vmem = pl.BlockSpec(memory_space=pltpu.VMEM)
    return pl.pallas_call(
        out_kernel,
        out_shape=(
            jax.ShapeDtypeStruct((half, D), f32),
            jax.ShapeDtypeStruct((half, D), bf16),
            jax.ShapeDtypeStruct((D, rows.shape[1]), bf16),
        ),
        in_specs=[vmem] + [pl.BlockSpec(memory_space=pl.ANY)] * 8,
        out_specs=(vmem, vmem, vmem),
        scratch_shapes=[pltpu.SemaphoreType.DMA((8,))],
        compiler_params=pltpu.CompilerParams(vmem_limit_bytes=58 * 1024 * 1024),
    )(rows, *pieces)


def turn(rows, cosine, sine, back=False):
    lane = lax.broadcasted_iota(jnp.int32, rows.shape, 1)
    other = jnp.where(lane % ROPE < ROPE // 2, -pltpu.roll(rows, 96, 1), pltpu.roll(rows, 32, 1))
    return rows * cosine - other * sine if back else rows * cosine + other * sine


def masked_scores(query, key, query_rope, key_rope):
    scores = (nt(query, key) + nt(query_rope, key_rope)) * (NOPE + ROPE) ** (-0.5)
    row = lax.broadcasted_iota(jnp.int32, scores.shape, 0)
    return jnp.where(row >= lax.broadcasted_iota(jnp.int32, scores.shape, 1), scores, -1e30)


def attend_kernel(
    first_ref,
    latent_ref,
    gain_ref,
    weight_ref,
    cosine_ref,
    sine_ref,
    norm_ref,
    query_ref,
    kv_ref,
    rope_ref,
    total_ref,
    context_ref,
):
    cosine, sine = cosine_ref[...], sine_ref[...]
    latent = latent_ref[...].astype(f32).T
    norm_ref[...] = (rms_parts(latent[:, :KVR])[0] * gain_ref[...]).astype(bf16)
    kv_ref[...] = nn(norm_ref[...], weight_ref[...]).astype(bf16)
    rope = turn(latent[:, KVR:], cosine, sine)
    ropes = (rope.astype(bf16), pltpu.roll(rope, ROPE, 1).astype(bf16))
    rope_ref[...] = ropes[0]
    heads = context_ref.shape[1] // VDIM
    query_ref[:, : heads * NOPE] = first_ref[:, : heads * NOPE].astype(bf16)
    totals = jnp.zeros(total_ref.shape, f32)
    lane = lax.broadcasted_iota(jnp.int32, totals.shape, 1)
    for n in range(heads):
        pair = slice(heads * NOPE + n // 2 * LANES, heads * NOPE + (n // 2 + 1) * LANES)
        if n % 2 == 0:
            query_ref[:, pair] = turn(first_ref[:, pair], cosine, sine).astype(bf16)
        key = slice(2 * n * NOPE, (2 * n + 1) * NOPE)
        value = slice((2 * n + 1) * NOPE, (2 * n + 2) * NOPE)
        own = slice(n * NOPE, (n + 1) * NOPE)
        scores = masked_scores(query_ref[:, own], kv_ref[:, key], query_ref[:, pair], ropes[n % 2])
        highest_score = jnp.max(scores, axis=1, keepdims=True)
        shifted = jnp.exp(scores - highest_score)
        total = jnp.sum(shifted, axis=1, keepdims=True)
        totals = jnp.where(lane == n, highest_score + jnp.log(total), totals)
        context_ref[:, own] = nn((shifted / total).astype(bf16), kv_ref[:, value]).astype(bf16)
    total_ref[...] = totals


def attend_step(first_out, latent, gain, weight, cosine, sine):
    rows = first_out.shape[0]
    vmem = pl.BlockSpec(memory_space=pltpu.VMEM)
    kv_width = weight.shape[1]
    heads = kv_width // (NOPE + VDIM)
    shapes = (
        ((rows, KVR), bf16),
        ((rows, heads * (NOPE + ROPE)), bf16),
        ((rows, kv_width), bf16),
        ((rows, LANES), bf16),
        ((rows, LANES), f32),
        ((rows, heads * VDIM), bf16),
    )
    return pl.pallas_call(
        attend_kernel,
        out_shape=tuple(jax.ShapeDtypeStruct(*shape) for shape in shapes),
        in_specs=[vmem] * 6,
        out_specs=(vmem,) * len(shapes),
        compiler_params=pltpu.CompilerParams(vmem_limit_bytes=58 * 1024 * 1024),
    )(first_out, latent, gain, weight, cosine, sine)


def attend_back_kernel(
    grad_ref,
    latent_ref,
    gain_ref,
    weight_ref,
    cosine_ref,
    sine_ref,
    query_ref,
    kv_ref,
    rope_ref,
    total_ref,
    grad_query_ref,
    grad_kv_ref,
    term_ref,
    gain_grad_ref,
):
    cosine, sine = cosine_ref[...], sine_ref[...]
    scale = (NOPE + ROPE) ** (-0.5)
    ropes = (rope_ref[...], pltpu.roll(rope_ref[...].astype(f32), ROPE, 1).astype(bf16))
    totals = total_ref[...]
    lane = lax.broadcasted_iota(jnp.int32, totals.shape, 1)
    heads = grad_ref.shape[1] // VDIM
    grad_ropes = [jnp.zeros(totals.shape, f32), jnp.zeros(totals.shape, f32)]
    grad_pair = None
    for n in range(heads):
        pair = slice(heads * NOPE + n // 2 * LANES, heads * NOPE + (n // 2 + 1) * LANES)
        key = slice(2 * n * NOPE, (2 * n + 1) * NOPE)
        value = slice((2 * n + 1) * NOPE, (2 * n + 2) * NOPE)
        own = slice(n * NOPE, (n + 1) * NOPE)
        scores = masked_scores(query_ref[:, own], kv_ref[:, key], query_ref[:, pair], ropes[n % 2])
        total = jnp.sum(jnp.where(lane == n, totals, 0.0), axis=1, keepdims=True)
        probabilities = jnp.exp(scores - total)
        grad_probs = nt(grad_ref[:, own], kv_ref[:, value])
        centred = jnp.sum(probabilities * grad_probs, axis=1, keepdims=True)
        grad_scores = (probabilities * (grad_probs - centred)).astype(bf16)
        grad_query_ref[:, own] = (nn(grad_scores, kv_ref[:, key]) * scale).astype(bf16)
        grad_kv_ref[:, key] = (tn(grad_scores, query_ref[:, own]) * scale).astype(bf16)
        grad_kv_ref[:, value] = tn(probabilities.astype(bf16), grad_ref[:, own]).astype(bf16)
        part = nn(grad_scores, ropes[n % 2]) * scale
        grad_pair = part if n % 2 == 0 else grad_pair + part
        if n % 2:
            grad_query_ref[:, pair] = turn(grad_pair, cosine, sine, True).astype(bf16)
        grad_ropes[n % 2] += tn(grad_scores, query_ref[:, pair]) * scale
    grad_rope = grad_ropes[0] + pltpu.roll(grad_ropes[1], ROPE, 1)
    grad_rope = turn(jnp.where(lane < ROPE, grad_rope, 0.0), cosine, sine, True)
    grad_norm = nt(grad_kv_ref[...], weight_ref[...])
    normed, inverse = rms_parts(latent_ref[:KVR, :].astype(f32).T)
    gain_grad_ref[...] = jnp.sum(grad_norm * normed, axis=0, keepdims=True)
    term_ref[:KVR, :] = rms_back(grad_norm, normed, inverse, gain_ref[...]).T
    term_ref[KVR:, :] = grad_rope.T


def attend_back_step(grad_context, latent, gain, weight, cosine, sine, query, kv, rope, totals):
    rows = grad_context.shape[0]
    vmem = pl.BlockSpec(memory_space=pltpu.VMEM)
    shapes = (
        (query.shape, bf16),
        (kv.shape, bf16),
        ((KVR + LANES, rows), f32),
        ((1, KVR), f32),
    )
    return pl.pallas_call(
        attend_back_kernel,
        out_shape=tuple(jax.ShapeDtypeStruct(*shape) for shape in shapes),
        in_specs=[vmem] * 10,
        out_specs=(vmem,) * len(shapes),
        compiler_params=pltpu.CompilerParams(vmem_limit_bytes=58 * 1024 * 1024),
    )(grad_context, latent, gain, weight, cosine, sine, query, kv, rope, totals)


def pack_kernel(place_ref, x_ref, query_ref, latent_ref, norm_ref, kv_ref, *refs):
    out_refs, kv_scr = refs[:8], refs[8]
    kv_scr[...] = tn(norm_ref[...], kv_ref[...]).astype(bf16)
    rows = x_ref.shape[1] // 8
    query = query_ref.shape[1]
    kv_rows = norm_ref.shape[1] // 8
    for j, out_ref in enumerate(out_refs):
        part = x_ref[:, j * rows : (j + 1) * rows]
        out_ref[:rows, :query] = tn(part, query_ref[...]).astype(bf16)
        out_ref[:rows, query:] = tn(part, latent_ref[...]).astype(bf16)
        start = pl.multiple_of(place_ref[j] * kv_rows, kv_rows)
        out_ref[rows:, :] = kv_scr[pl.ds(start, kv_rows), :]


def pack_step(places, rows, grad_query, grad_latent, latent_norm, grad_kv):
    vmem = pl.BlockSpec(memory_space=pltpu.VMEM)
    width = grad_kv.shape[1]
    count = (rows.shape[1] + latent_norm.shape[1]) // 8
    grad_latent = jnp.pad(
        grad_latent, ((0, 0), (0, width - grad_query.shape[1] - grad_latent.shape[1]))
    )
    return pl.pallas_call(
        pack_kernel,
        out_shape=(jax.ShapeDtypeStruct((count, width), bf16),) * 8,
        in_specs=[pl.BlockSpec(memory_space=pltpu.SMEM)] + [vmem] * 5,
        out_specs=(vmem,) * 8,
        scratch_shapes=[pltpu.VMEM((latent_norm.shape[1], width), bf16)],
        compiler_params=pltpu.CompilerParams(vmem_limit_bytes=58 * 1024 * 1024),
    )(places, rows, grad_query, grad_latent, latent_norm, grad_kv)


def dense_shards(*arrays):
    return dense_layer(*arrays)


def dense_layer(
    block_input,
    cotangent,
    norm1_gain,
    latent_gain,
    norm2_gain,
    w_query,
    w_latent,
    w_kv,
    w_out,
    expert_gate,
    expert_up,
    expert_down,
    shared_gate,
    shared_up,
    shared_down,
    routed_expert_index,
    slots,
    gate_weights,
):
    f = lax.axis_index(FSDP)
    h = lax.axis_index(HEADS)
    t = lax.axis_index(TENSOR)
    row_count = block_input.shape[0]
    head_dim = NOPE + ROPE
    local_heads = w_query.shape[1] // head_dim
    query_width = local_heads * head_dim
    hosts = lax.axis_size(FSDP) * lax.axis_size(HEADS)
    experts = EXP_LOC * hosts
    capacity = row_count * TOP * 5 // (4 * experts)

    relative = [(f ^ dx) * 4 + (t + k) % 4 for dx in range(2) for k in range(4)]
    absolute = [(F ^ f) * 4 + (T - t) % 4 for F in range(2) for T in range(4)]
    turns = (0, 2, 1, 3)

    def chunks_to(array, order, axis):
        return jnp.concatenate([pick(array, i, 8, axis) for i in order], axis=axis)

    def quarter(array):
        return pick(array, h, 4, 0)

    def rows_relative(array):
        return jnp.concatenate([pick(array, h ^ j, 4, 0) for j in turns], axis=0)

    def rows_absolute(array):
        places = [h ^ i for i in range(4)]
        return jnp.concatenate([pick(array, (p % 2) * 2 + p // 2, 4, 0) for p in places], axis=0)

    def reduce_heads(kept, sent):
        summed = kept + swap_heads(sent.astype(bf16), 1).astype(f32)
        half = summed.shape[0] // 2
        return summed[:half] + swap_heads(summed[half:].astype(bf16), 2).astype(f32)

    def gather_heads(own):
        near = jnp.concatenate([own, swap_heads(own, 2)], axis=0)
        return jnp.concatenate([near, swap_heads(near, 1)], axis=0)

    query_rows = w_query.shape[0]
    latent_width = w_latent.shape[1] // 4
    latent_stop = query_width + latent_width
    kv_width = w_kv.shape[1]

    def fill(piece, axis, size):
        return jnp.pad(piece, [(0, size - piece.shape[axis] if a == axis else 0) for a in range(2)])

    by_head = w_query.reshape(query_rows, local_heads, head_dim)
    first_pack = jnp.concatenate(
        [
            by_head[..., :NOPE].reshape(query_rows, -1),
            by_head[..., NOPE:].reshape(query_rows, -1),
            pick(w_latent, h, 4, 1),
        ],
        axis=1,
    )
    first_pack = jnp.concatenate([fill(first_pack, 1, kv_width), w_kv], axis=0)
    first_along, first_far = gather_weight(first_pack)
    first_parts = first_along + first_far

    own_ids, own_slots, own_gates = quarter(routed_expert_index), quarter(slots), quarter(gate_weights)
    lanes = jnp.arange(LANES)[None, None, :]
    used_route = (own_ids[:, :, None] == lanes) & (own_slots[:, :, None] < capacity)
    route_weights = jnp.sum(jnp.where(used_route, own_gates[:, :, None].astype(f32), 0.0), axis=1)
    cotangent_own = quarter(cotangent)
    grad_unit = jnp.concatenate([cotangent_own, route_weights.astype(bf16)], axis=1)

    hidden = expert_gate.shape[2]
    part = -(-hidden // LANES) * LANES
    shared_own = lax.all_to_all(
        jnp.stack([shared_gate.T, shared_up.T, shared_down]),
        PLANE,
        split_axis=1,
        concat_axis=2,
        tiled=True,
    )
    shared_hidden = shared_own.shape[1]

    def side_by_side(routed):
        return jnp.pad(routed, ((0, 0), (0, part - hidden), (0, 0))).reshape(-1, D)

    gate_all = side_by_side(jnp.swapaxes(expert_gate, 1, 2))
    up_all = side_by_side(jnp.swapaxes(expert_up, 1, 2))
    shared_own = after(shared_own, first_along[1], first_along[3])
    shared_all = jnp.concatenate([fill(shared_own[i], 0, LANES) for i in range(2)], axis=0)
    down_all = jnp.concatenate([side_by_side(expert_down), fill(shared_own[2], 0, LANES)], axis=0)

    residual = chunks_to(block_input, relative, 1).astype(f32)
    gain1 = chunks_to(norm1_gain, relative, 0)
    first_normed, first_inverse = rms_parts(residual)
    first_input = (first_normed * gain1).astype(bf16)
    cosine, sine_table = (jnp.tile(a, (1, LANES * 2 // ROPE)) for a in rope_tables(row_count))
    first_input = after(first_input, gate_all, up_all, shared_all, down_all)
    places = jnp.stack(relative).astype(jnp.int32)
    first_out, w_first, kv_full = first_step(places, first_input, first_parts, w_kv.shape[0])
    w_queries, w_latents = w_first[:, :query_width], w_first[:, query_width:latent_stop]
    latent_own = first_out[:, query_width:latent_stop].astype(bf16).T
    latent_raw = rows_absolute(gather_heads(latent_own))
    latent_raw = fill(latent_raw, 0, KVR + LANES)
    latent_gain = latent_gain[None, :]
    tables = (latent_raw, latent_gain, kv_full, cosine, sine_table)
    latent_norm, *saved, context = attend_step(first_out, *tables)
    out_along, out_far = gather_weight(w_out.T)
    context = rows_relative(context)
    kept, sent, out_full = out_step(context, out_along + out_far)
    attention_own = reduce_heads(kept, sent)
    after_attention = quarter(block_input).astype(f32) + chunks_to(attention_own, absolute, 1)
    second_normed, second_inverse = rms_parts(after_attention)
    second_input = (second_normed * norm2_gain).astype(bf16)

    rows = gather_rows(second_input)
    grads = gather_rows(grad_unit)
    first_expert = ((f * lax.axis_size(HEADS) + h) * EXP_LOC).astype(jnp.int32).reshape(1)
    out_groups = []
    grad_groups, hidden_parts, gate_parts, up_parts, shared_parts = [], [], [], [], []
    for rows_g, grads_g in zip(rows, grads):
        near, far, out_near, out_far, hidden_g, gate_g, up_g, shared_g = hidden_step(
            first_expert, rows_g, grads_g, gate_all, up_all, shared_all, down_all
        )
        grad_groups.append((near, far))
        out_groups.append((out_near, out_far))
        hidden_parts.append(hidden_g)
        gate_parts.append(gate_g)
        up_parts.append(up_g)
        shared_parts.append(shared_g)
    grad_second = scatter_rows(grad_groups, [grad_groups[3][0]])

    second_gain_part = jnp.sum(grad_second * second_normed, axis=0)
    grad_after = cotangent_own.astype(f32) + rms_back(
        grad_second, second_normed, second_inverse, norm2_gain
    )
    grad_after = chunks_to(grad_after, relative, 1)
    grad_attention = gather_heads(grad_after.astype(bf16))
    out_part = tn(grad_attention, context)
    grad_context = nn(grad_attention, out_full).astype(bf16)
    grad_context = rows_absolute(grad_context)
    grad_query_raw, grad_key_value, latent_term, latent_gain_part = attend_back_step(
        grad_context, *tables, *saved
    )
    latent_gain_part = latent_gain_part[0]
    first_from_query = nt(rows_relative(grad_query_raw), w_queries)
    latent_term = rows_relative(latent_term[: 4 * latent_width])
    half = latent_term.shape[0] // 2
    grad_latent = reduce_heads(latent_term[:half], latent_term[half:]).astype(bf16)
    grad_latent_rows = jnp.concatenate([pick(grad_latent, h ^ j, 4, 1) for j in turns], axis=1)
    first_from_latent = lax.dot_general(
        grad_latent_rows, w_latents, (((0,), (1,)), ((), ())), preferred_element_type=f32
    )
    first_pieces = pack_step(
        places, first_input, grad_query_raw, grad_latent.T, latent_norm, grad_key_value
    )
    grad_first = reduce_heads(
        first_from_query[: row_count // 2] + first_from_latent[: row_count // 2],
        first_from_query[row_count // 2 :] + first_from_latent[row_count // 2 :],
    )
    first_normed_own = quarter(first_normed)
    first_gain_part = jnp.sum(grad_first * first_normed_own, axis=0)
    input_own = grad_after + rms_back(grad_first, first_normed_own, quarter(first_inverse), gain1)
    input_grad = rows_absolute(gather_heads(chunks_to(input_own.astype(bf16), absolute, 1))).astype(f32)

    w_out_grad = scatter_weight(out_part.reshape(8, -1, out_part.shape[1]), end=grad_first).T
    first_grad = scatter_weight(first_pieces, grad_first)
    w_query_grad = jnp.concatenate(
        [
            first_grad[:query_rows, : local_heads * NOPE].reshape(query_rows, local_heads, NOPE),
            first_grad[:query_rows, local_heads * NOPE : query_width].reshape(
                query_rows, local_heads, ROPE
            ),
        ],
        axis=2,
    ).reshape(query_rows, query_width)
    w_kv_grad = first_grad[query_rows:]
    gain_parts = jnp.concatenate(
        [
            first_gain_part.reshape(8, -1),
            chunks_to(second_gain_part, relative, 0).reshape(8, -1),
            chunks_to(latent_gain_part, relative, 0).reshape(8, -1),
        ],
        axis=1,
    ).reshape(8, -1, latent_width)
    gain_parts = scatter_weight(gain_parts)
    last = jnp.concatenate([first_grad[:query_rows, query_width:latent_stop], gain_parts], axis=0)
    last = rows_absolute(gather_heads(last.astype(bf16))).reshape(4, -1, latent_width).astype(f32)
    latent_rows = w_latent.shape[0]
    w_latent_grad = jnp.concatenate([last[i, :latent_rows] for i in range(4)], axis=1)
    gains = jnp.sum(last[:, latent_rows:], axis=0).reshape(-1)
    side = D // 8

    out_groups = [tuple(after(p, grad_after) for p in pair) for pair in out_groups]
    ffn_own = scatter_rows(out_groups)
    output = rows_absolute(gather_heads((after_attention + ffn_own).astype(bf16)))
    rows_list = [p for g in rows for p in g]
    grads_list = [p for g in grads for p in g]
    routed = EXP_LOC * part
    shared_grads = shared_grad(shared_parts, hidden_parts, rows_list, grads_list, routed, shared_hidden)
    shared_grads = lax.all_to_all(
        after(shared_grads, grad_query_raw), PLANE, split_axis=0, concat_axis=0, tiled=True
    ).reshape(8, 3, shared_hidden, -1)
    shared_grads = [shared_grads[:, i].astype(f32).reshape(8 * shared_hidden, -1) for i in range(3)]
    expert_grads = []
    for lefts, rights in ((gate_parts, rows_list), (up_parts, rows_list), (hidden_parts, grads_list)):
        expert_grads.append(weight_grad(lefts, rights, 0, routed, (EXP_LOC, hidden, D)))
    return (
        output,
        input_grad,
        gains[:side],
        gains[2 * side :],
        gains[side : 2 * side],
        w_query_grad,
        w_latent_grad,
        w_kv_grad,
        w_out_grad,
        jnp.swapaxes(expert_grads[0], 1, 2),
        jnp.swapaxes(expert_grads[1], 1, 2),
        expert_grads[2],
        shared_grads[0].T,
        shared_grads[1].T,
        shared_grads[2],
    )


def solution(mesh):
    in_specs = (
        P((FSDP, TENSOR), None),
        P((FSDP, TENSOR), None),
        P(),
        P(),
        P(),
        P((FSDP, TENSOR), HEADS),
        P((FSDP, TENSOR), None),
        P((FSDP, TENSOR), HEADS),
        P(HEADS, (FSDP, TENSOR)),
        P((FSDP, HEADS), None, TENSOR),
        P((FSDP, HEADS), None, TENSOR),
        P((FSDP, HEADS), TENSOR, None),
        P((FSDP, HEADS), TENSOR),
        P((FSDP, HEADS), TENSOR),
        P(TENSOR, (FSDP, HEADS)),
        P((FSDP, TENSOR), None),
        P((FSDP, TENSOR), None),
        P((FSDP, TENSOR), None),
    )
    out_specs = (
        P((FSDP, TENSOR), None),
        P((FSDP, TENSOR), None),
        P((FSDP, TENSOR)),
        P((FSDP, TENSOR)),
        P((FSDP, TENSOR)),
        P((FSDP, TENSOR), HEADS),
        P((FSDP, TENSOR), None),
        P((FSDP, TENSOR), HEADS),
        P(HEADS, (FSDP, TENSOR)),
        P((FSDP, HEADS), None, TENSOR),
        P((FSDP, HEADS), None, TENSOR),
        P((FSDP, HEADS), TENSOR, None),
        P((FSDP, HEADS), TENSOR),
        P((FSDP, HEADS), TENSOR),
        P(TENSOR, (FSDP, HEADS)),
    )
    dense = tuple(mesh.shape[a] for a in (FSDP, HEADS, TENSOR)) == (2, 4, 4)
    program = dense_shards if dense else shards
    program = jax.shard_map(
        program, mesh=mesh, in_specs=in_specs, out_specs=out_specs, check_vma=False
    )
    return program
```
